32 devices in a mesh: groups: 2 (over y), ctx: 4 (over z), tp: 2 (over x), fsdp: 2 (over core).
Axes of the slice: x: 2, y: 2, z: 4, core: 2. Of those that a mesh axis runs over, the one named last changes fastest.
Arguments:
- x_in: bfloat16 [3072, 16384], P(('groups', 'ctx'), ('tp', 'fsdp')), parts along dimension 0, may hold values from -6 to 6
- bc_in: bfloat16 [3072, 8, 512], P(('groups', 'ctx'), ('tp', 'fsdp')), parts along dimension 0, may hold values from -4 to 4
- z_in: bfloat16 [3072, 16384], P(('groups', 'ctx'), ('tp', 'fsdp')), parts along dimension 0, may hold values from -6 to 6
- dt_in: bfloat16 [3072, 256], P(('groups', 'ctx'), ('tp', 'fsdp')), parts along dimension 0, may hold values from -6 to 6
- conv_x: float32 [4, 16384], P(None, ('tp', 'fsdp')), may hold values from -3 to 3
- conv_bc: float32 [4, 8, 512], P(None, ('tp', 'fsdp')), may hold values from -3 to 3
- dt_bias: float32 [256], P(('tp', 'fsdp')), may hold values from -0.3 to 0.3
- a_log: float32 [256], P(('tp', 'fsdp')), as said below
- d_skip: float32 [256], P(('tp', 'fsdp')), may hold values from 0.5 to 2
- norm_gain: float32 [16384], P(('tp', 'fsdp')), may hold values from 0.5 to 1.5
Outputs:
- mixed: bfloat16 [3072, 16384], P(('groups', 'ctx'), ('tp', 'fsdp')), parts along dimension 0
The draws below stay inside these ranges and needn't reach their ends.
There are 2 independent parts, one for each index of `groups`. The reference program is written for one: setup_inputs(seed, part) draws one part's arguments, and reference() takes and returns one part's arrays. A program takes and returns all parts, laid end to end along the dimension named above; an argument that names none is the same for every part. Nothing has to cross between parts.
Inputs may be any that keep to these rules, and one draw needn't show every extreme that they name: a_log lies between log(1.6 / 1536) and -2.8.
All inputs are finite; a program needn't handle non-finite values.
Results may differ from the reference program's by a relative error of at most 0.0062.
Values may be sent and summed in bfloat16 or wider, within the bound.
No kernel may reach another device: no remote copies, remote signals or barrier semaphores. Data moves between devices by JAX's collectives and lax.ppermute only.
A program may use at most 128 MiB of HBM per device.

```python
import math
import jax
import jax.numpy as jnp
from jax import lax

HEADS = 256
HEAD_DIM = 64
STATE = 256
GROUPS = 8
KERNEL = 4
TOK_DEV = 384
TOKENS = 1536


def draw_a_log(key, part):
    first_key, second_key, third_key = jax.random.split(jax.random.fold_in(key, 17), 3)
    share = 0.5
    slow_pick = jax.random.uniform(first_key, (HEADS,), jnp.float32) < share
    slow_value = jnp.log(jax.random.uniform(second_key, (HEADS,), jnp.float32, minval=1.6, maxval=2.2) / TOKENS)
    fast_value = jax.random.uniform(third_key, (HEADS,), jnp.float32, minval=-3.5, maxval=-2.8)
    return jnp.where(slow_pick, slow_value, fast_value).astype(jnp.float32)


def block_levels(rng, dims, cuts, low, high):
    def one(axis_at, parts):
        steps = jax.random.uniform(jax.random.fold_in(jax.random.fold_in(rng, 6), axis_at), (parts,), jnp.float32, low / len(cuts), high / len(cuts))
        return jnp.repeat(jnp.exp(steps), dims[axis_at] // parts).reshape((-1,) + (1,) * (len(dims) - axis_at - 1))

    loudness = one(*cuts[0])
    for cut in cuts[1:]:
        loudness = loudness * one(*cut)
    return loudness


def centred(own_key, shape, scale, limit, cuts=(), held_as=jnp.bfloat16):
    values = scale * jax.random.normal(own_key, shape, jnp.float32)
    if cuts:
        values = values * block_levels(own_key, shape, cuts, -0.22, 0.18)
    return jnp.clip(values, -limit, limit).astype(held_as)


def setup_inputs(seed: int = 0, part: int = 0) -> dict:
    arg_keys = jax.random.split(jax.random.key(seed), 11)
    part_splits = jax.random.split(jax.random.fold_in(arg_keys[10], part), 11)
    x_in = centred(part_splits[0], (TOKENS, HEADS * HEAD_DIM), 1.0, 6.0, ((0, 4), (1, 4)))
    bc_in = centred(part_splits[1], (TOKENS, GROUPS, 2 * STATE), 0.3, 4.0, ((0, 4), (1, 4)))
    z_in = centred(part_splits[2], (TOKENS, HEADS * HEAD_DIM), 1.0, 6.0, ((0, 4), (1, 4)))
    dt_in = centred(part_splits[3], (TOKENS, HEADS), 0.5, 6.0, ((0, 4), (1, 4)))
    conv_x = centred(arg_keys[4], (KERNEL, HEADS * HEAD_DIM), KERNEL ** -0.5, 3.0, ((1, 4),), jnp.float32)
    conv_bc = centred(arg_keys[5], (KERNEL, GROUPS, 2 * STATE), KERNEL ** -0.5, 3.0, ((1, 4),), jnp.float32)
    dt_bias = jnp.clip(jax.random.uniform(arg_keys[6], (HEADS,), jnp.float32, -0.3, 0.3) * block_levels(arg_keys[6], (HEADS,), ((0, 4),), -0.4, 0.0), -0.3, 0.3)
    a_log = draw_a_log(jax.random.fold_in(arg_keys[10], 71), part)
    d_skip = jnp.clip(0.5 + 1.5 * jax.random.uniform(arg_keys[8], (HEADS,), jnp.float32) ** block_levels(arg_keys[8], (HEADS,), ((0, 4),), -0.2, 0.2), 0.5, 2.0)
    norm_gain = jnp.clip(1.0 + 0.1 * jax.random.normal(arg_keys[9], (HEADS * HEAD_DIM,), jnp.float32), 0.5, 1.5)
    return dict(x_in=x_in, bc_in=bc_in, z_in=z_in, dt_in=dt_in, conv_x=conv_x, conv_bc=conv_bc, dt_bias=dt_bias, a_log=a_log, d_skip=d_skip, norm_gain=norm_gain)


def product(form, left, right):
    left = lax.optimization_barrier(left)
    right = lax.optimization_barrier(right)
    return jnp.einsum(form, left.astype(jnp.float32), right.astype(jnp.float32), precision=lax.Precision.HIGHEST)

def causal_conv(current, earlier, kernel_taps):
    length = current.shape[0]
    joined = jnp.concatenate([earlier, current], axis=0)
    summed = jnp.zeros(current.shape, jnp.float32)
    for offset in range(kernel_taps.shape[0]):
        summed = summed + kernel_taps[offset] * joined[offset:offset + length]
    return jax.nn.silu(summed).astype(jnp.bfloat16)

def span_terms(inputs_x, b_rows, c_rows, steps_dt, rates, skip_gain):
    length, heads, width = inputs_x.shape
    groups = b_rows.shape[1]
    per_group = heads // groups
    block = math.gcd(per_group, 8)
    cumulative = jnp.cumsum(-rates * steps_dt, axis=0)
    scores = product('tgn,sgn->gts', c_rows, b_rows)
    causal = lax.broadcasted_iota(jnp.int32, (length, length), 0) >= lax.broadcasted_iota(jnp.int32, (length, length), 1)

    def diagonal_block(start):
        grid = lax.dynamic_index_in_dim(scores, start // per_group, 0, keepdims=False)
        cum_block = lax.dynamic_slice_in_dim(cumulative, start, block, 1).T
        dt_block = lax.dynamic_slice_in_dim(steps_dt, start, block, 1).T
        x_block = lax.dynamic_slice_in_dim(inputs_x, start, block, 1)
        spread = cum_block[:, :, None] - cum_block[:, None, :]
        decay = jnp.where(causal, jnp.exp(jnp.minimum(spread, 0.0)), 0.0)
        mixing = (grid[None] * decay * dt_block[:, None, :]).astype(jnp.bfloat16)
        return product('hts,shp->thp', mixing, x_block)
    starts = jnp.arange(0, heads, block, dtype=jnp.int32)
    blocks = lax.map(diagonal_block, starts)
    diag_part = jnp.moveaxis(blocks, 0, 1).reshape(length, heads, width)
    final_log = cumulative[-1]
    to_end = jnp.exp(final_log[None, :] - cumulative) * steps_dt
    weighted = (inputs_x * to_end[:, :, None]).astype(jnp.bfloat16).reshape(length, groups, per_group, width)
    state = product('sghp,sgn->ghpn', weighted, b_rows).reshape(heads, width, b_rows.shape[2])
    local_out = diag_part + skip_gain[None, :, None] * inputs_x
    return (local_out, state, final_log, cumulative)

def carried_term(c_rows, cumulative, incoming):
    length, groups, depth = c_rows.shape
    heads = incoming.shape[0]
    width = incoming.shape[1]
    rounded = incoming.astype(jnp.bfloat16).reshape(groups, heads // groups, width, depth)
    term = product('tgn,ghpn->tghp', c_rows, rounded).reshape(length, heads, width)
    return term * jnp.exp(cumulative)[:, :, None]

def gated_norm(ssm_out, gate_in, gain_row, groups):
    length = ssm_out.shape[0]
    gated = ssm_out.astype(jnp.float32) * jax.nn.silu(gate_in.astype(jnp.float32))
    shaped = gated.reshape(length, groups, -1)
    scale = lax.rsqrt(lax.optimization_barrier(jnp.mean(shaped * shaped, axis=-1, keepdims=True)) + 1e-05)
    return ((shaped * scale).reshape(length, -1) * gain_row).astype(jnp.bfloat16)

def reference(x_in, bc_in, z_in, dt_in, conv_x, conv_bc, dt_bias, a_log, d_skip, norm_gain):
    spans = x_in.shape[0] // TOK_DEV
    margin = KERNEL - 1
    rates = jnp.exp(a_log)

    def advance(carry, pieces):
        incoming, earlier_x, earlier_bc = carry
        now_x, now_bc, now_z, now_dt = pieces
        conv_out = causal_conv(now_x, earlier_x, conv_x).reshape(TOK_DEV, HEADS, HEAD_DIM)
        bc_out = causal_conv(now_bc, earlier_bc, conv_bc)
        steps_dt = jax.nn.softplus(now_dt.astype(jnp.float32) + dt_bias)
        local_out, state, final_log, cumulative = span_terms(conv_out, bc_out[:, :, :STATE], bc_out[:, :, STATE:], steps_dt, rates, d_skip)
        ssm_out = (local_out + carried_term(bc_out[:, :, STATE:], cumulative, incoming)).astype(jnp.bfloat16)
        ssm_out = ssm_out.reshape(TOK_DEV, HEADS * HEAD_DIM)
        following = jnp.exp(final_log)[:, None, None] * incoming + state
        return ((following, now_x[-margin:], now_bc[-margin:]), gated_norm(ssm_out, now_z, norm_gain, GROUPS))
    initial = (jnp.zeros((HEADS, HEAD_DIM, STATE), jnp.float32), jnp.zeros((margin, HEADS * HEAD_DIM), jnp.bfloat16), jnp.zeros((margin, GROUPS, 2 * STATE), jnp.bfloat16))
    pieces = (x_in.reshape(spans, TOK_DEV, HEADS * HEAD_DIM), bc_in.reshape(spans, TOK_DEV, GROUPS, 2 * STATE), z_in.reshape(spans, TOK_DEV, HEADS * HEAD_DIM), dt_in.reshape(spans, TOK_DEV, HEADS))
    ended, outputs = lax.scan(advance, initial, pieces)
    return outputs.reshape(spans * TOK_DEV, HEADS * HEAD_DIM)
```

```python
import functools

import jax
import jax.numpy as jnp
from jax import lax
from jax.experimental import pallas as pl
from jax.experimental.pallas import tpu as pltpu
from jax.sharding import PartitionSpec as P

HEAD_DIM = 64
STATE = 256
KERNEL = 4
SUB = 128
CHUNK = 512
F32 = jnp.float32
BF16 = jnp.bfloat16


def dot(left, right):
    return jnp.dot(left, right, preferred_element_type=F32)


def silu(value):
    half = 0.5 * value
    return half + half * jnp.tanh(half)


def two_terms(value):
    high = value.astype(BF16)
    low = (value - high.astype(F32)).astype(BF16)
    return high, low


def causal_conv(current, earlier, taps):
    length, width = current.shape
    wide = current.astype(F32)
    head = jnp.concatenate([jnp.zeros((8 - KERNEL + 1, width), F32), earlier.astype(F32)], axis=0)
    joined = jnp.concatenate([head, wide], axis=0)
    total = taps[KERNEL - 1 : KERNEL] * wide
    for back in range(1, KERNEL):
        row = KERNEL - 1 - back
        total = total + taps[row : row + 1] * joined[8 - back : 8 - back + length]
    return silu(total).astype(BF16)


def prepare_kernel(
    groups, bc_ref, early_ref, taps_ref, dt_ref, bias_ref, rate_ref, skip_ref,
    left_ref, bt_ref, u_ref, v_ref, rows_ref,
):
    length, heads = dt_ref.shape
    shifted = dt_ref[...].astype(F32) + bias_ref[...]
    steps = jnp.maximum(shifted, 0.0) + jnp.log1p(jnp.exp(-jnp.abs(shifted)))
    log_decay = -jnp.exp(rate_ref[...]) * steps
    at = lax.broadcasted_iota(jnp.int32, (length, length), 0)
    of = lax.broadcasted_iota(jnp.int32, (length, length), 1)
    lower = jnp.where(at >= of, 1.0, 0.0).astype(BF16)
    first = log_decay.astype(BF16)
    rest = log_decay - first.astype(F32)
    second = rest.astype(BF16)
    third = (rest - second.astype(F32)).astype(BF16)
    cumulative = dot(lower, first) + dot(lower, second) + dot(lower, third)
    subs = length // SUB
    decays, scales = [], []
    start = jnp.zeros((1, heads), F32)
    for sub in range(subs):
        rows = slice(sub * SUB, (sub + 1) * SUB)
        inside = cumulative[rows] - start
        for ref, value in ((u_ref, jnp.exp(inside)), (v_ref, jnp.exp(-inside) * steps[rows])):
            high, low = two_terms(value)
            ref[rows, :] = jnp.concatenate([high, low], axis=1)
        end = cumulative[(sub + 1) * SUB - 1 : (sub + 1) * SUB]
        decays.append(jnp.exp(end - start))
        scales.append(jnp.exp(start))
        start = end
    lines = decays + scales + [skip_ref[...], jnp.exp(start)]
    lines = lines + [jnp.zeros((1, heads), F32)] * (rows_ref.shape[0] - len(lines))
    high, low = two_terms(jnp.concatenate(lines, axis=0))
    rows_ref[...] = jnp.concatenate([high, low], axis=1)
    causal = at[:SUB, :SUB] >= of[:SUB, :SUB]
    for group in range(groups):
        lanes = slice(group * 2 * STATE, (group + 1) * 2 * STATE)
        conv = causal_conv(bc_ref[:, lanes], early_ref[:, lanes], taps_ref[:, lanes])
        b_turned = conv[:, :STATE].astype(F32).T.astype(BF16)
        c_rows = conv[:, STATE:]
        bt_ref[group] = b_turned
        for sub in range(subs):
            rows = slice(sub * SUB, (sub + 1) * SUB)
            scores = jnp.where(causal, dot(c_rows[rows], b_turned[:, rows]), 0.0)
            left_ref[group, rows, :SUB] = scores.astype(BF16)
            left_ref[group, rows, SUB:] = c_rows[rows]


def local_kernel(
    first_head, x_ref, early_ref, taps_ref, z_ref, left_ref, bt_ref, u_ref, v_ref, rows_ref,
    part_ref, reach_ref, state_ref, send_ref, lanes_ref,
):
    length, width = x_ref.shape
    terms = u_ref.shape[1]
    row = lax.broadcasted_iota(jnp.int32, (terms, width), 0)
    lane = lax.broadcasted_iota(jnp.int32, (terms, width), 1)
    heads = terms // 2
    owner = jnp.where(row >= heads, row - heads, row) - first_head
    spread = jnp.where(
        (lane >= owner * HEAD_DIM) & (lane < (owner + 1) * HEAD_DIM), 1.0, 0.0
    ).astype(BF16)
    lanes = dot(rows_ref[...], spread)
    lanes_ref[...] = lanes
    conv = causal_conv(x_ref[...], early_ref[...], taps_ref[...])
    subs = length // SUB
    skip = lanes[2 * subs : 2 * subs + 1]
    state = None
    for sub in range(subs):
        rows = slice(sub * SUB, (sub + 1) * SUB)
        inputs = conv[rows].astype(F32)
        scaled = (inputs * dot(v_ref[rows], spread)).astype(BF16)
        decay = lanes[sub : sub + 1]
        added = dot(bt_ref[0, :, rows], scaled)
        if sub == 0:
            inner = dot(left_ref[0, rows, :SUB], scaled)
            state = decay * added
        else:
            inner = dot(left_ref[0, rows, :SUB], scaled) + dot(
                left_ref[0, rows, SUB:], state.astype(BF16)
            )
            state = decay * (state + added)
        grown = dot(u_ref[rows], spread)
        gate = silu(z_ref[rows].astype(F32))
        part_ref[rows, :] = gate * (grown * inner + skip * inputs)
        reach_ref[rows, :] = gate * grown * lanes[subs + sub : subs + sub + 1]
    state_ref[...] = state
    send_ref[...] = state.astype(send_ref.dtype)


def finish_kernel(chunks, *refs):
    left_ref, gain_ref = refs[0], refs[1]
    parts = refs[2 : 2 + chunks]
    reaches = refs[2 + chunks : 2 + 2 * chunks]
    carried = refs[2 + 2 * chunks : 2 + 3 * chunks]
    latest = refs[2 + 3 * chunks : 2 + 4 * chunks]
    out_ref = refs[-1]
    c_rows = left_ref[0, :, SUB:]
    gated, square = [], None
    for index in range(chunks):
        incoming = (carried[index][...].astype(F32) + latest[index][...].astype(F32)).astype(BF16)
        value = parts[index][...] + reaches[index][...] * dot(c_rows, incoming)
        gated.append(value)
        term = jnp.sum(value * value, axis=1, keepdims=True)
        square = term if square is None else square + term
    width = gated[0].shape[1]
    scale = lax.rsqrt(square * (1.0 / (width * chunks)) + 1e-05)
    for index in range(chunks):
        lanes = slice(index * width, (index + 1) * width)
        out_ref[:, lanes] = (gated[index] * scale * gain_ref[:, lanes]).astype(BF16)


def whole(shape):
    return pl.BlockSpec(shape, lambda *_: (0,) * len(shape))


def shards(x_in, bc_in, z_in, dt_in, conv_x, conv_bc, dt_bias, a_log, d_skip, norm_gain):
    length, channels = x_in.shape
    groups = bc_in.shape[1]
    heads = channels // HEAD_DIM
    contexts = lax.axis_size("ctx")
    wire = BF16 if contexts <= 8 else F32
    margin = KERNEL - 1
    subs = length // SUB
    ahead = [(i, i + 1) for i in range(contexts - 1)]
    bc_flat = bc_in.reshape(length, groups * 2 * STATE)
    early_x, early_bc = lax.ppermute((x_in[-margin:], bc_flat[-margin:]), "ctx", ahead)
    line_rows = -(-(2 * subs + 2) // 8) * 8
    sub_width = SUB + STATE
    left, b_turned, grow, shrink, lines = pl.pallas_call(
        functools.partial(prepare_kernel, groups),
        out_shape=(
            jax.ShapeDtypeStruct((groups, length, sub_width), BF16),
            jax.ShapeDtypeStruct((groups, STATE, length), BF16),
            jax.ShapeDtypeStruct((length, 2 * heads), BF16),
            jax.ShapeDtypeStruct((length, 2 * heads), BF16),
            jax.ShapeDtypeStruct((line_rows, 2 * heads), BF16),
        ),
        name="prepare",
    )(
        bc_flat, early_bc, conv_bc.reshape(KERNEL, groups * 2 * STATE), dt_in,
        dt_bias.reshape(1, heads), a_log.reshape(1, heads), d_skip.reshape(1, heads),
    )

    per_group = channels // groups
    in_group = per_group // CHUNK
    count = channels // CHUNK
    local = []
    for chunk in range(count):
        group = chunk // in_group

        def column(rows, chunk=chunk):
            return pl.BlockSpec((rows, CHUNK), lambda i: (0, chunk))

        def grouped(rows, width, group=group):
            return pl.BlockSpec((1, rows, width), lambda i: (group, 0, 0))

        local.append(
            pl.pallas_call(
                functools.partial(local_kernel, chunk * (CHUNK // HEAD_DIM)),
                grid=(1,),
                in_specs=[
                    column(length), column(margin), column(KERNEL), column(length),
                    grouped(length, sub_width), grouped(STATE, length),
                    whole((length, 2 * heads)), whole((length, 2 * heads)),
                    whole((line_rows, 2 * heads)),
                ],
                out_specs=[
                    whole((length, CHUNK)), whole((length, CHUNK)), whole((STATE, CHUNK)),
                    whole((STATE, CHUNK)), whole((line_rows, CHUNK)),
                ],
                out_shape=(
                    jax.ShapeDtypeStruct((length, CHUNK), F32),
                    jax.ShapeDtypeStruct((length, CHUNK), F32),
                    jax.ShapeDtypeStruct((STATE, CHUNK), F32),
                    jax.ShapeDtypeStruct((STATE, CHUNK), wire),
                    jax.ShapeDtypeStruct((line_rows, CHUNK), F32),
                ),
                compiler_params=pltpu.CompilerParams(vmem_limit_bytes=24 << 20),
                cost_estimate=pl.CostEstimate(
                    flops=2 * length * CHUNK * 800, bytes_accessed=4 << 20,
                    transcendentals=2 * length * CHUNK,
                ),
                name="local",
            )(x_in, early_x, conv_x, z_in, left, b_turned, grow, shrink, lines)
        )

    carried, latest = [], []
    for chunk in range(count):
        state, sent, lanes = local[chunk][2:]
        total = lanes[2 * subs + 1 : 2 * subs + 2]
        received = []
        for hop in range(contexts - 1):
            arrived = lax.ppermute(sent, "ctx", [(hop, hop + 1)])
            received.append(arrived)
            sent = (total * arrived.astype(F32) + state).astype(wire)
        before = received[0]
        for arrived in received[1:-1]:
            before = before + arrived
        carried.append(before)
        latest.append(received[-1] if contexts > 2 else jnp.zeros_like(before))

    rows = 128
    gain = norm_gain.reshape(1, channels)
    out = None
    for group in range(groups):
        picked = range(group * in_group, (group + 1) * in_group)
        tall = pl.BlockSpec((rows, CHUNK), lambda i: (i, 0))
        operands = [left, gain]
        operands += [local[c][0] for c in picked] + [local[c][1] for c in picked]
        operands += [carried[c] for c in picked] + [latest[c] for c in picked]
        specs = [
            pl.BlockSpec((1, rows, sub_width), lambda i, group=group: (group, i, 0)),
            pl.BlockSpec((1, per_group), lambda i, group=group: (0, group)),
        ]
        specs += [tall] * (2 * in_group) + [whole((STATE, CHUNK))] * (2 * in_group)
        aliases = {}
        if out is not None:
            aliases = {len(operands): 0}
            operands.append(out)
            specs.append(pl.BlockSpec(memory_space=pl.ANY))
        out = pl.pallas_call(
            functools.partial(finish_kernel, in_group),
            grid=(length // rows,),
            in_specs=specs,
            out_specs=pl.BlockSpec((rows, per_group), lambda i, group=group: (i, group)),
            out_shape=jax.ShapeDtypeStruct((length, channels), BF16),
            input_output_aliases=aliases,
            compiler_params=pltpu.CompilerParams(vmem_limit_bytes=32 << 20),
            cost_estimate=pl.CostEstimate(
                flops=2 * length * per_group * STATE, bytes_accessed=8 << 20, transcendentals=length
            ),
            name="finish",
        )(*operands)
    return out


def solution(mesh):
    placed = (
        P(("groups", "ctx"), ("tp", "fsdp")),
        P(("groups", "ctx"), ("tp", "fsdp"), None),
        P(("groups", "ctx"), ("tp", "fsdp")),
        P(("groups", "ctx"), ("tp", "fsdp")),
        P(None, ("tp", "fsdp")),
        P(None, ("tp", "fsdp"), None),
        P(("tp", "fsdp")),
        P(("tp", "fsdp")),
        P(("tp", "fsdp")),
        P(("tp", "fsdp")),
    )
    return jax.shard_map(
        shards,
        mesh=mesh,
        in_specs=placed,
        out_specs=P(("groups", "ctx"), ("tp", "fsdp")),
        check_vma=False,
    )
```

```python
import functools

import jax
import jax.numpy as jnp
from jax import lax
from jax.experimental import pallas as pl
from jax.experimental.pallas import tpu as pltpu
from jax.sharding import PartitionSpec as P

HEAD_DIM = 64
STATE = 256
KERNEL = 4
SUB = 128
CHUNK = 512
LOCAL_VMEM = 16 << 20
LAG = 1
F32 = jnp.float32
BF16 = jnp.bfloat16


def dot(left, right):
    return jnp.dot(left, right, preferred_element_type=F32)


def silu(value):
    half = 0.5 * value
    return half + half * jnp.tanh(half)


def two_terms(value):
    high = value.astype(BF16)
    low = (value - high.astype(F32)).astype(BF16)
    return high, low


def causal_conv(current, earlier, taps):
    length, width = current.shape
    wide = current.astype(F32)
    head = jnp.concatenate([jnp.zeros((8 - KERNEL + 1, width), F32), earlier.astype(F32)], axis=0)
    joined = jnp.concatenate([head, wide], axis=0)
    total = taps[KERNEL - 1 : KERNEL] * wide
    for back in range(1, KERNEL):
        row = KERNEL - 1 - back
        total = total + taps[row : row + 1] * joined[8 - back : 8 - back + length]
    return silu(total).astype(BF16)


def column_of(row):
    size = row.shape[1]
    at = lax.broadcasted_iota(jnp.int32, (size, size), 0)
    of = lax.broadcasted_iota(jnp.int32, (size, size), 1)
    return jnp.sum(jnp.where(at == of, row, 0.0), axis=1, keepdims=True)


def terms_by_row(value):
    high = value.astype(BF16).astype(F32)
    low = value - high
    return jnp.concatenate([high, low], axis=0).T.astype(BF16)


def steps_kernel(staged, *refs):
    whole_refs = refs[:staged]
    small_refs = refs[staged : staged + 4]
    copies_out = refs[staged + 4 : 2 * staged + 4]
    u_ref, v_ref, rows_ref = refs[2 * staged + 4 : 2 * staged + 7]
    small = refs[2 * staged + 7 : 2 * staged + 11]
    small_sems, whole_sems = refs[2 * staged + 11 :]
    small_copies = [
        pltpu.make_async_copy(source, target, small_sems.at[index])
        for index, (source, target) in enumerate(zip(small_refs, small))
    ]
    whole_copies = [
        pltpu.make_async_copy(source, target, whole_sems.at[index])
        for index, (source, target) in enumerate(zip(whole_refs, copies_out))
    ]
    for copy in small_copies + whole_copies:
        copy.start()
    for copy in small_copies:
        copy.wait()
    dt_ref, bias_ref, rate_ref, skip_ref = small
    heads, length = dt_ref.shape
    shifted = dt_ref[...].astype(F32) + column_of(bias_ref[...])
    steps = jnp.maximum(shifted, 0.0) + jnp.log1p(jnp.exp(-jnp.abs(shifted)))
    log_decay = -jnp.exp(column_of(rate_ref[...])) * steps
    of = lax.broadcasted_iota(jnp.int32, (length, length), 0)
    at = lax.broadcasted_iota(jnp.int32, (length, length), 1)
    upper = jnp.where(at >= of, 1.0, 0.0).astype(BF16)
    first = log_decay.astype(BF16)
    rest = log_decay - first.astype(F32)
    second = rest.astype(BF16)
    third = (rest - second.astype(F32)).astype(BF16)
    cumulative = dot(first, upper) + dot(second, upper) + dot(third, upper)
    subs = length // SUB
    decays, scales = [], []
    start = jnp.zeros((heads, 1), F32)
    for sub in range(subs):
        rows = slice(sub * SUB, (sub + 1) * SUB)
        inside = cumulative[:, rows] - start
        u_ref[rows, :] = terms_by_row(jnp.exp(inside))
        v_ref[rows, :] = terms_by_row(jnp.exp(-inside) * steps[:, rows])
        end = cumulative[:, (sub + 1) * SUB - 1 : (sub + 1) * SUB]
        decays.append(jnp.exp(end - start))
        scales.append(jnp.exp(start))
        start = end
    lines = decays + scales + [column_of(skip_ref[...]), jnp.exp(start)]
    lane = lax.broadcasted_iota(jnp.int32, (heads, SUB), 1)
    table = jnp.zeros((heads, SUB), F32)
    for index, line in enumerate(lines):
        table = jnp.where(lane == index, line, table)
    rows_ref[...] = terms_by_row(table)[: rows_ref.shape[0]]
    for copy in whole_copies:
        copy.wait()


def groups_kernel(groups, bc_ref, early_ref, taps_ref, gate_ref, left_ref, bt_ref):
    length = bc_ref.shape[0]
    subs = length // SUB
    of = lax.broadcasted_iota(jnp.int32, (SUB, SUB), 1)
    at = lax.broadcasted_iota(jnp.int32, (SUB, SUB), 0)
    causal = at >= of
    for group in range(groups):
        lanes = slice(group * 2 * STATE, (group + 1) * 2 * STATE)
        conv = causal_conv(bc_ref[:, lanes], early_ref[:, lanes], taps_ref[:, group, :])
        b_turned = conv[:, :STATE].astype(F32).T.astype(BF16)
        c_rows = conv[:, STATE:]
        bt_ref[group] = b_turned
        for sub in range(subs):
            rows = slice(sub * SUB, (sub + 1) * SUB)
            scores = jnp.where(causal, dot(c_rows[rows], b_turned[:, rows]), 0.0)
            left_ref[group, rows, :SUB] = scores.astype(BF16)
            left_ref[group, rows, SUB:] = c_rows[rows]


def local_kernel(
    first_head, x_ref, early_ref, taps_ref, z_ref, left_ref, bt_ref, u_ref, v_ref, rows_ref, *refs
):
    part_ref, reach_ref, state_ref, send_ref, lanes_ref = refs[-5:]
    length, width = x_ref.shape
    terms = u_ref.shape[1]
    row = lax.broadcasted_iota(jnp.int32, (terms, width), 0)
    lane = lax.broadcasted_iota(jnp.int32, (terms, width), 1)
    heads = terms // 2
    owner = jnp.where(row >= heads, row - heads, row) - first_head
    spread = jnp.where(
        (lane >= owner * HEAD_DIM) & (lane < (owner + 1) * HEAD_DIM), 1.0, 0.0
    ).astype(BF16)
    lanes = dot(rows_ref[...], spread)
    lanes_ref[...] = lanes
    conv = causal_conv(x_ref[...], early_ref[...], taps_ref[...])
    subs = length // SUB
    skip = lanes[2 * subs : 2 * subs + 1]
    state = None
    for sub in range(subs):
        rows = slice(sub * SUB, (sub + 1) * SUB)
        inputs = conv[rows].astype(F32)
        scaled = (inputs * dot(v_ref[rows], spread)).astype(BF16)
        decay = lanes[sub : sub + 1]
        added = dot(bt_ref[0, :, rows], scaled)
        if sub == 0:
            inner = dot(left_ref[0, rows, :SUB], scaled)
            state = decay * added
        else:
            inner = dot(left_ref[0, rows, :SUB], scaled) + dot(
                left_ref[0, rows, SUB:], state.astype(BF16)
            )
            state = decay * (state + added)
        grown = dot(u_ref[rows], spread)
        gate = silu(z_ref[rows].astype(F32))
        part_ref[rows, :] = gate * (grown * inner + skip * inputs)
        reach_ref[rows, :] = gate * grown * lanes[subs + sub : subs + sub + 1]
    state_ref[...] = state
    send_ref[...] = state.astype(send_ref.dtype)


def combine_kernel(line, lanes_ref, state_ref, arrived_ref, gate_ref, sent_ref):
    total = lanes_ref[line : line + 1]
    joined = total * arrived_ref[...].astype(F32) + state_ref[...]
    sent_ref[...] = joined.astype(sent_ref.dtype)


def absorb_kernel(left_ref, part_ref, reach_ref, before_ref, latest_ref, gate_ref, gated_ref, square_ref):
    length, width = part_ref.shape
    incoming = (before_ref[...].astype(F32) + latest_ref[...].astype(F32)).astype(BF16)
    for start in range(0, length, SUB):
        rows = slice(start, start + SUB)
        value = part_ref[rows] + reach_ref[rows] * dot(left_ref[0, rows, SUB:], incoming)
        gated_ref[rows, :] = value
        power = value * value
        total = power[:, :128]
        for lane in range(128, width, 128):
            total = total + power[:, lane : lane + 128]
        square_ref[rows, :] = total


def finish_kernel(chunks, *refs):
    gain_ref = refs[0]
    gated = refs[1 : 1 + chunks]
    squares = refs[1 + chunks : 1 + 2 * chunks]
    out_ref = refs[-1]
    width = gated[0].shape[1]
    total = squares[0][...]
    for square in squares[1:]:
        total = total + square[...]
    mean = jnp.sum(total, axis=1, keepdims=True) * (1.0 / (width * chunks))
    scale = lax.rsqrt(mean + 1e-05)
    for index in range(chunks):
        lanes = slice(index * width, (index + 1) * width)
        out_ref[:, lanes] = (gated[index][...] * scale * gain_ref[:, lanes]).astype(BF16)


def whole(shape):
    return pl.BlockSpec(shape, lambda *_: (0,) * len(shape))


def shards(x_in, bc_in, z_in, dt_in, conv_x, conv_bc, dt_bias, a_log, d_skip, norm_gain):
    length, channels = x_in.shape
    groups = bc_in.shape[1]
    heads = channels // HEAD_DIM
    contexts = lax.axis_size("ctx")
    wire = BF16 if contexts <= 8 else F32
    margin = KERNEL - 1
    subs = length // SUB
    ahead = [(i, i + 1) for i in range(contexts - 1)]
    bc_width = groups * 2 * STATE
    bc_flat = lax.optimization_barrier(bc_in.reshape(length, bc_width))
    early = jnp.concatenate([x_in[-margin:], bc_flat[-margin:]], axis=1)
    early = lax.ppermute(early, "ctx", ahead)
    line_rows = -(-(2 * subs + 2) // 8) * 8
    sub_width = SUB + STATE
    staged = (x_in, z_in, conv_x, conv_bc, norm_gain.reshape(1, channels))
    small = (dt_in.T, dt_bias.reshape(1, heads), a_log.reshape(1, heads), d_skip.reshape(1, heads))
    x_in, z_in, taps_x, taps_bc, gain, grow, shrink, lines = pl.pallas_call(
        functools.partial(steps_kernel, len(staged)),
        in_specs=[pl.BlockSpec(memory_space=pltpu.HBM)] * (len(staged) + len(small)),
        out_specs=tuple(pl.BlockSpec(memory_space=pltpu.VMEM) for _ in range(len(staged) + 3)),
        out_shape=tuple(jax.ShapeDtypeStruct(array.shape, array.dtype) for array in staged) + (
            jax.ShapeDtypeStruct((length, 2 * heads), BF16),
            jax.ShapeDtypeStruct((length, 2 * heads), BF16),
            jax.ShapeDtypeStruct((line_rows, 2 * heads), BF16),
        ),
        scratch_shapes=[pltpu.VMEM(array.shape, array.dtype) for array in small] + [
            pltpu.SemaphoreType.DMA((len(small),)), pltpu.SemaphoreType.DMA((len(staged),)),
        ],
        compiler_params=pltpu.CompilerParams(vmem_limit_bytes=12 << 20),
        cost_estimate=pl.CostEstimate(
            flops=6 * heads * length * length, bytes_accessed=8 << 20, transcendentals=1 << 18
        ),
        name="steps",
    )(*[pltpu.with_memory_space_constraint(array, pltpu.HBM) for array in staged + small])
    left, b_turned = pl.pallas_call(
        functools.partial(groups_kernel, groups),
        out_shape=(
            jax.ShapeDtypeStruct((groups, length, sub_width), BF16),
            jax.ShapeDtypeStruct((groups, STATE, length), BF16),
        ),
        grid=(1,),
        in_specs=[
            whole((length, bc_width)),
            pl.BlockSpec((margin, bc_width), lambda i: (0, channels // bc_width)),
            whole((KERNEL, groups, 2 * STATE)), whole((line_rows, 2 * heads)),
        ],
        out_specs=(whole((groups, length, sub_width)), whole((groups, STATE, length))),
        compiler_params=pltpu.CompilerParams(vmem_limit_bytes=12 << 20),
        cost_estimate=pl.CostEstimate(
            flops=4 * groups * length * SUB * STATE, bytes_accessed=4 << 20,
            transcendentals=length * bc_width,
        ),
        name="groups",
    )(bc_flat, early, taps_bc, lines)

    per_group = channels // groups
    in_group = per_group // CHUNK
    count = channels // CHUNK
    token = pl.BlockSpec((8, 128), lambda i: (0, 0))

    def local(chunk, gates):
        group = chunk // in_group

        def column(rows):
            return pl.BlockSpec((rows, CHUNK), lambda i: (0, chunk))

        def grouped(rows, width):
            return pl.BlockSpec((1, rows, width), lambda i: (group, 0, 0))

        return pl.pallas_call(
            functools.partial(local_kernel, chunk * (CHUNK // HEAD_DIM)),
            grid=(1,),
            in_specs=[
                column(length), column(margin), column(KERNEL), column(length),
                grouped(length, sub_width), grouped(STATE, length),
                whole((length, 2 * heads)), whole((length, 2 * heads)),
                whole((line_rows, 2 * heads)),
            ] + [token] * len(gates),
            out_specs=[
                whole((length, CHUNK)), whole((length, CHUNK)), whole((STATE, CHUNK)),
                whole((STATE, CHUNK)), whole((line_rows, CHUNK)),
            ],
            out_shape=(
                jax.ShapeDtypeStruct((length, CHUNK), F32),
                jax.ShapeDtypeStruct((length, CHUNK), F32),
                jax.ShapeDtypeStruct((STATE, CHUNK), F32),
                jax.ShapeDtypeStruct((STATE, CHUNK), wire),
                jax.ShapeDtypeStruct((line_rows, CHUNK), F32),
            ),
            compiler_params=pltpu.CompilerParams(vmem_limit_bytes=LOCAL_VMEM),
            cost_estimate=pl.CostEstimate(
                flops=2 * length * CHUNK * 800, bytes_accessed=4 << 20,
                transcendentals=2 * length * CHUNK,
            ),
            name="local",
        )(x_in, early, taps_x, z_in, left, b_turned, grow, shrink, lines, *gates)

    def combine(lanes, state, came, gate):
        return pl.pallas_call(
            functools.partial(combine_kernel, 2 * subs + 1),
            grid=(1,),
            in_specs=[whole((line_rows, CHUNK)), whole((STATE, CHUNK)), whole((STATE, CHUNK)), token],
            out_specs=whole((STATE, CHUNK)),
            out_shape=jax.ShapeDtypeStruct((STATE, CHUNK), wire),
            compiler_params=pltpu.CompilerParams(vmem_limit_bytes=4 << 20),
            cost_estimate=pl.CostEstimate(
                flops=2 * STATE * CHUNK, bytes_accessed=1 << 20, transcendentals=0
            ),
            name="combine",
        )(lanes, state, came, gate)

    def absorb(chunk, before, latest, gate):
        group = chunk // in_group
        part, reach = pieces[chunk][:2]
        return pl.pallas_call(
            absorb_kernel,
            grid=(1,),
            in_specs=[
                pl.BlockSpec((1, length, sub_width), lambda i: (group, 0, 0)),
                whole((length, CHUNK)), whole((length, CHUNK)),
                whole((STATE, CHUNK)), whole((STATE, CHUNK)), token,
            ],
            out_specs=(whole((length, CHUNK)), whole((length, 128))),
            out_shape=(
                jax.ShapeDtypeStruct((length, CHUNK), F32),
                jax.ShapeDtypeStruct((length, 128), F32),
            ),
            compiler_params=pltpu.CompilerParams(vmem_limit_bytes=8 << 20),
            cost_estimate=pl.CostEstimate(
                flops=2 * length * CHUNK * STATE, bytes_accessed=3 << 20, transcendentals=0
            ),
            name="absorb",
        )(left, part, reach, before, latest, gate)

    def finish(group, done, out, gate):
        rows = SUB
        tall = pl.BlockSpec((rows, CHUNK), lambda i: (i, 0))
        thin = pl.BlockSpec((rows, 128), lambda i: (i, 0))
        operands = [gain] + [pair[0] for pair in done] + [pair[1] for pair in done] + [gate]
        specs = [pl.BlockSpec((1, per_group), lambda i: (0, group))]
        specs += [tall] * in_group + [thin] * in_group + [token]
        aliases = {}
        if out is not None:
            aliases = {len(operands): 0}
            operands.append(out)
            specs.append(pl.BlockSpec(memory_space=pl.ANY))
        return pl.pallas_call(
            functools.partial(finish_kernel, in_group),
            grid=(length // rows,),
            in_specs=specs,
            out_specs=pl.BlockSpec((rows, per_group), lambda i: (i, group)),
            out_shape=jax.ShapeDtypeStruct((length, channels), BF16),
            input_output_aliases=aliases,
            compiler_params=pltpu.CompilerParams(vmem_limit_bytes=12 << 20),
            cost_estimate=pl.CostEstimate(
                flops=4 * length * per_group, bytes_accessed=4 << 20, transcendentals=length
            ),
            name="finish",
        )(*operands)

    hops = contexts - 1
    pieces, done = [], []
    arrived = [[] for _ in range(hops)]
    gate, out = None, None
    for step in range(count + LAG * hops):
        if step < count:
            piece = local(step, [] if gate is None else [gate])
            pieces.append(piece)
            gate = piece[4]
            arrived[0].append(lax.ppermute(piece[3], "ctx", [(0, 1)]))
        for hop in range(1, hops):
            chunk = step - LAG * hop
            if 0 <= chunk < count:
                state, lanes = pieces[chunk][2], pieces[chunk][4]
                gate = combine(lanes, state, arrived[hop - 1][chunk], gate)
                arrived[hop].append(lax.ppermute(gate, "ctx", [(hop, hop + 1)]))
        chunk = step - LAG * hops
        if 0 <= chunk < count:
            before = arrived[0][chunk]
            for hop in range(1, hops - 1):
                before = before + arrived[hop][chunk]
            latest = arrived[-1][chunk] if hops > 1 else jnp.zeros_like(before)
            done.append(absorb(chunk, before, latest, gate))
            gate = done[-1][1]
            if (chunk + 1) % in_group == 0:
                group = chunk // in_group
                out = finish(group, done[group * in_group :], out, gate)
    return out


def solution(mesh):
    placed = (
        P(("groups", "ctx"), ("tp", "fsdp")),
        P(("groups", "ctx"), ("tp", "fsdp"), None),
        P(("groups", "ctx"), ("tp", "fsdp")),
        P(("groups", "ctx"), ("tp", "fsdp")),
        P(None, ("tp", "fsdp")),
        P(None, ("tp", "fsdp"), None),
        P(("tp", "fsdp")),
        P(("tp", "fsdp")),
        P(("tp", "fsdp")),
        P(("tp", "fsdp")),
    )
    return jax.shard_map(
        shards,
        mesh=mesh,
        in_specs=placed,
        out_specs=P(("groups", "ctx"), ("tp", "fsdp")),
        check_vma=False,
    )
```

```python
import functools

import jax
import jax.numpy as jnp
from jax import lax
from jax.experimental import pallas as pl
from jax.experimental.pallas import tpu as pltpu
from jax.sharding import PartitionSpec as P

HEAD_DIM = 64
STATE = 256
KERNEL = 4
SUB = 128
CHUNK = 512
PIECE = 2 * CHUNK
LOCAL_VMEM = 16 << 20
COST = pl.CostEstimate(flops=1 << 10, bytes_accessed=1 << 10, transcendentals=0)
F32 = jnp.float32
BF16 = jnp.bfloat16


def dot(left, right):
    return jnp.dot(left, right, preferred_element_type=F32)


def silu(value):
    half = 0.5 * value
    return half + half * jnp.tanh(half)


def two_terms(value):
    high = value.astype(BF16)
    low = (value - high.astype(F32)).astype(BF16)
    return high, low


def causal_conv(current, earlier, taps):
    length, width = current.shape
    wide = current.astype(F32)
    head = jnp.concatenate([jnp.zeros((8 - KERNEL + 1, width), F32), earlier.astype(F32)], axis=0)
    joined = jnp.concatenate([head, wide], axis=0)
    total = taps[KERNEL - 1 : KERNEL] * wide
    for back in range(1, KERNEL):
        row = KERNEL - 1 - back
        total = total + taps[row : row + 1] * joined[8 - back : 8 - back + length]
    return silu(total).astype(BF16)


def column_of(row):
    size = row.shape[1]
    at = lax.broadcasted_iota(jnp.int32, (size, size), 0)
    of = lax.broadcasted_iota(jnp.int32, (size, size), 1)
    return jnp.sum(jnp.where(at == of, row, 0.0), axis=1, keepdims=True)


def terms_by_row(value):
    high = value.astype(BF16).astype(F32)
    low = value - high
    return jnp.concatenate([high, low], axis=0).T.astype(BF16)


def started(pairs, sems):
    copies = [
        pltpu.make_async_copy(source, target, sems.at[index])
        for index, (source, target) in enumerate(pairs)
    ]
    for copy in copies:
        copy.start()
    return copies


def staging(stages, sources, targets, sems):
    return started(
        [
            (source.at[:, piece * PIECE : (piece + 1) * PIECE], target)
            for piece, source, target in zip(stages, sources, targets)
        ],
        sems,
    )


def steps_kernel(
    x_hbm, taps_x_hbm, taps_bc_hbm, bc_hbm, gain_hbm, dt_hbm, bias_hbm, rate_hbm, skip_hbm,
    x_ref, tail_ref, taps_x_ref, taps_bc_ref, bc_ref, gain_ref, u_ref, v_ref, rows_ref, *scratch
):
    small, (small_sems, whole_sems) = scratch[:4], scratch[4:]
    small_copies = started(zip((dt_hbm, bias_hbm, rate_hbm, skip_hbm), small), small_sems)
    tall, wide = x_ref.shape[0], x_ref.shape[1]
    whole_copies = started(
        (
            (x_hbm.at[tall - 8 : tall, :], tail_ref), (bc_hbm, bc_ref), (taps_bc_hbm, taps_bc_ref),
            (taps_x_hbm, taps_x_ref), (x_hbm.at[:, :wide], x_ref), (gain_hbm, gain_ref),
        ),
        whole_sems,
    )
    for copy in small_copies:
        copy.wait()
    dt_ref, bias_ref, rate_ref, skip_ref = small
    heads, length = dt_ref.shape
    shifted = dt_ref[...].astype(F32) + column_of(bias_ref[...])
    steps = jnp.maximum(shifted, 0.0) + jnp.log1p(jnp.exp(-jnp.abs(shifted)))
    log_decay = -jnp.exp(column_of(rate_ref[...])) * steps
    of = lax.broadcasted_iota(jnp.int32, (length, length), 0)
    at = lax.broadcasted_iota(jnp.int32, (length, length), 1)
    upper = jnp.where(at >= of, 1.0, 0.0).astype(BF16)
    first = log_decay.astype(BF16)
    rest = log_decay - first.astype(F32)
    second = rest.astype(BF16)
    third = (rest - second.astype(F32)).astype(BF16)
    cumulative = dot(first, upper) + dot(second, upper) + dot(third, upper)
    subs = length // SUB
    decays, scales = [], []
    start = jnp.zeros((heads, 1), F32)
    for sub in range(subs):
        rows = slice(sub * SUB, (sub + 1) * SUB)
        inside = cumulative[:, rows] - start
        u_ref[rows, :] = terms_by_row(jnp.exp(inside))
        v_ref[rows, :] = terms_by_row(jnp.exp(-inside) * steps[:, rows])
        end = cumulative[:, (sub + 1) * SUB - 1 : (sub + 1) * SUB]
        decays.append(jnp.exp(end - start))
        scales.append(jnp.exp(start))
        start = end
    lines = decays + scales + [column_of(skip_ref[...]), jnp.exp(start)]
    lane = lax.broadcasted_iota(jnp.int32, (heads, SUB), 1)
    table = jnp.zeros((heads, SUB), F32)
    for index, line in enumerate(lines):
        table = jnp.where(lane == index, line, table)
    rows_ref[...] = terms_by_row(table)[: rows_ref.shape[0]]
    for copy in whole_copies:
        copy.wait()


def stage_kernel(stages, gate_ref, *refs):
    for copy in staging(stages, refs[: len(stages)], refs[len(stages) : -1], refs[-1]):
        copy.wait()


def groups_kernel(groups, stages, bc_ref, early_ref, taps_ref, gate_ref, *refs):
    sources, (left_ref, bt_ref), targets = refs[: len(stages)], refs[len(stages) : len(stages) + 2], refs[len(stages) + 2 : -1]
    copies = staging(stages, sources, targets, refs[-1])
    length = bc_ref.shape[0]
    subs = length // SUB
    of = lax.broadcasted_iota(jnp.int32, (SUB, SUB), 1)
    at = lax.broadcasted_iota(jnp.int32, (SUB, SUB), 0)
    causal = at >= of
    for group in range(groups):
        lanes = slice(group * 2 * STATE, (group + 1) * 2 * STATE)
        base = early_ref.shape[1] - bc_ref.shape[1] + lanes.start
        earlier = early_ref[:, base : base + 2 * STATE]
        conv = causal_conv(bc_ref[:, lanes], earlier, taps_ref[:, group, :])
        b_turned = conv[:, :STATE].astype(F32).T.astype(BF16)
        c_rows = conv[:, STATE:]
        bt_ref[group] = b_turned
        for sub in range(subs):
            rows = slice(sub * SUB, (sub + 1) * SUB)
            scores = jnp.where(causal, dot(c_rows[rows], b_turned[:, rows]), 0.0)
            left_ref[group, rows, :SUB] = scores.astype(BF16)
            left_ref[group, rows, SUB:] = c_rows[rows]
    for copy in copies:
        copy.wait()


def spread_matrix(terms, width, first_head):
    row = lax.broadcasted_iota(jnp.int32, (terms, width), 0)
    lane = lax.broadcasted_iota(jnp.int32, (terms, width), 1)
    heads = terms // 2
    start = (jnp.where(row >= heads, row - heads, row) - first_head) * HEAD_DIM
    return jnp.where((lane >= start) & (lane < start + HEAD_DIM), 1.0, 0.0).astype(BF16)


def next_state(state, scaled, b_turned, decay):
    added = dot(b_turned, scaled)
    return decay * (added if state is None else state + added)


def first_kernel(
    group, chunk, stages, place_ref, x_ref, taps_ref, v_ref, rows_ref, bc_ref, bc_taps_ref, gate_ref, *refs
):
    send_ref = refs[len(stages)]
    copies = staging(stages, refs[: len(stages)], refs[len(stages) + 1 : -1], refs[-1]) if stages else []

    @pl.when(place_ref[0] == 0)
    def _():
        at = slice(chunk * CHUNK, (chunk + 1) * CHUNK)
        length, width = x_ref.shape[0], CHUNK
        spread = spread_matrix(v_ref.shape[1], width, chunk * (CHUNK // HEAD_DIM))
        lanes = dot(rows_ref[...], spread)
        start = group * 2 * STATE
        nothing = jnp.zeros((KERNEL - 1, STATE), BF16)
        b_rows = causal_conv(bc_ref[:, start : start + STATE], nothing, bc_taps_ref[:, group, :STATE])
        b_turned = b_rows.astype(F32).T.astype(BF16)
        nothing = jnp.zeros((KERNEL - 1, width), BF16)
        inner_at = slice(chunk * CHUNK % PIECE, chunk * CHUNK % PIECE + CHUNK)
        conv = causal_conv(x_ref[:, inner_at], nothing, taps_ref[:, at])
        state = None
        for sub in range(length // SUB):
            rows = slice(sub * SUB, (sub + 1) * SUB)
            scaled = (conv[rows].astype(F32) * dot(v_ref[rows], spread)).astype(BF16)
            state = next_state(state, scaled, b_turned[:, rows], lanes[sub : sub + 1])
        send_ref[...] = state.astype(send_ref.dtype)

    for copy in copies:
        copy.wait()


def local_kernel(
    group, chunk, stages, x_ref, early_ref, taps_ref, z_ref, left_ref, bt_ref, u_ref, v_ref, rows_ref,
    gate_ref, *refs
):
    outs = len(stages)
    part_ref, reach_ref, state_ref, lanes_ref = refs[outs : outs + 4]
    copies = staging(stages, refs[:outs], refs[outs + 4 : -1], refs[-1]) if stages else []
    lanes_at = slice(chunk * CHUNK, (chunk + 1) * CHUNK)
    inner_at = slice(chunk * CHUNK % PIECE, chunk * CHUNK % PIECE + CHUNK)
    length, width = x_ref.shape[0], CHUNK
    spread = spread_matrix(u_ref.shape[1], width, chunk * (CHUNK // HEAD_DIM))
    lanes = dot(rows_ref[...], spread)
    lanes_ref[...] = lanes
    conv = causal_conv(x_ref[:, inner_at], early_ref[:, lanes_at], taps_ref[:, lanes_at])
    subs = length // SUB
    skip = lanes[2 * subs : 2 * subs + 1]
    state = None
    for sub in range(subs):
        rows = slice(sub * SUB, (sub + 1) * SUB)
        inputs = conv[rows].astype(F32)
        scaled = (inputs * dot(v_ref[rows], spread)).astype(BF16)
        inner = dot(left_ref[group, rows, :SUB], scaled)
        if sub > 0:
            inner = inner + dot(left_ref[group, rows, SUB:], state.astype(BF16))
        state = next_state(state, scaled, bt_ref[group, :, rows], lanes[sub : sub + 1])
        grown = dot(u_ref[rows], spread)
        gate = silu(z_ref[rows, inner_at].astype(F32))
        part_ref[rows, :] = gate * (grown * inner + skip * inputs)
        reach_ref[rows, :] = gate * grown * lanes[subs + sub : subs + sub + 1]
    state_ref[...] = state
    for copy in copies:
        copy.wait()


def combine_kernel(line, owners, arrivals, place_ref, *refs):
    place = place_ref[0]
    lanes = refs[: len(owners)]
    states = refs[len(owners) : 2 * len(owners)]
    came = refs[2 * len(owners) : 2 * len(owners) + arrivals]
    sent_ref = refs[-1]
    total, state = lanes[0][line : line + 1], states[0][...]
    for owner, lane_ref, state_ref in zip(owners[1:], lanes[1:], states[1:]):
        total = jnp.where(place >= owner, lane_ref[line : line + 1], total)
        state = jnp.where(place >= owner, state_ref[...], state)
    value = came[0][...].astype(F32)
    for other in came[1:]:
        value = jnp.where(place >= 2, other[...].astype(F32), value)
    sent_ref[...] = (total * value + state).astype(sent_ref.dtype)


def absorb_kernel(group, owners, left_ref, part_ref, reach_ref, place_ref, *refs):
    length, width = part_ref.shape
    gated_ref, square_ref = refs[-2:]
    place = place_ref[0]
    incoming = refs[0][...].astype(F32)
    for owner, other in zip(owners[1:], refs[1:]):
        incoming = jnp.where(place >= owner, other[...].astype(F32), incoming)
    incoming = incoming.astype(BF16)
    for start in range(0, length, SUB):
        rows = slice(start, start + SUB)
        value = part_ref[rows] + reach_ref[rows] * dot(left_ref[group, rows, SUB:], incoming)
        gated_ref[rows, :] = value
        power = value * value
        total = power[:, :128]
        for lane in range(128, width, 128):
            total = total + power[:, lane : lane + 128]
        square_ref[rows, :] = total


def finish_kernel(group, chunks, gain_ref, *refs):
    gated = refs[:chunks]
    squares = refs[chunks : 2 * chunks]
    out_ref = refs[-1]
    height = out_ref.shape[0]
    rows = pl.ds(pl.multiple_of(pl.program_id(0) * height, height), height)
    total = squares[0][rows, :]
    for square in squares[1:]:
        total = total + square[rows, :]
    mean = jnp.sum(total, axis=1, keepdims=True) * (1.0 / (CHUNK * chunks))
    scale = lax.rsqrt(mean + 1e-05)
    for index in range(chunks):
        lanes = slice(index * CHUNK, (index + 1) * CHUNK)
        start = (group * chunks + index) * CHUNK
        out_ref[:, lanes] = (gated[index][rows, :] * scale * gain_ref[:, start : start + CHUNK]).astype(BF16)


def shards(x_in, bc_in, z_in, dt_in, conv_x, conv_bc, dt_bias, a_log, d_skip, norm_gain):
    length, channels = x_in.shape
    groups = bc_in.shape[1]
    heads = channels // HEAD_DIM
    contexts = lax.axis_size("ctx")
    wire = BF16 if contexts <= 8 else F32
    margin = KERNEL - 1
    subs = length // SUB
    ahead = [(i, i + 1) for i in range(contexts - 1)]
    bc_width = groups * 2 * STATE
    line_rows = -(-(2 * subs + 2) // 8) * 8
    sub_width = SUB + STATE
    place = lax.axis_index("ctx").astype(jnp.int32).reshape(1)
    small = (dt_in.T, dt_bias.reshape(1, heads), a_log.reshape(1, heads), d_skip.reshape(1, heads))
    far = lambda array: pltpu.with_memory_space_constraint(array, pltpu.HBM)
    large = tuple(far(array) for array in (x_in, conv_x, conv_bc, bc_in, norm_gain.reshape(1, channels)))
    begun = PIECE
    x_begun, tail, taps_x, taps_bc, bc_near, gain, grow, shrink, lines = pl.pallas_call(
        steps_kernel,
        in_specs=[pl.BlockSpec(memory_space=pltpu.HBM)] * (len(large) + len(small)),
        out_specs=[pl.BlockSpec(memory_space=pltpu.VMEM)] * 9,
        out_shape=(
            jax.ShapeDtypeStruct((length, begun), BF16),
            jax.ShapeDtypeStruct((8, channels), BF16),
            jax.ShapeDtypeStruct(conv_x.shape, F32),
            jax.ShapeDtypeStruct(conv_bc.shape, F32),
            jax.ShapeDtypeStruct(bc_in.shape, BF16),
            jax.ShapeDtypeStruct((1, channels), F32),
            jax.ShapeDtypeStruct((length, 2 * heads), BF16),
            jax.ShapeDtypeStruct((length, 2 * heads), BF16),
            jax.ShapeDtypeStruct((line_rows, 2 * heads), BF16),
        ),
        scratch_shapes=[pltpu.VMEM(array.shape, array.dtype) for array in small] + [
            pltpu.SemaphoreType.DMA((len(small),)), pltpu.SemaphoreType.DMA((6,)),
        ],
        compiler_params=pltpu.CompilerParams(vmem_limit_bytes=12 << 20),
        cost_estimate=COST,
        name="steps",
    )(*large, *[far(array) for array in small])
    bc_flat = bc_near.reshape(length, bc_width)
    per_group = channels // groups
    in_group = per_group // CHUNK
    count = channels // CHUNK
    hops = contexts - 1
    near = pl.BlockSpec(memory_space=pltpu.VMEM)
    scalar = pl.BlockSpec(memory_space=pltpu.SMEM)
    afar = pl.BlockSpec(memory_space=pltpu.HBM)
    last_piece = channels // PIECE - 1
    hold = jax.ShapeDtypeStruct((STATE, CHUNK), wire)
    from_first, from_later = [], []

    def send(value):
        from_first.append(lax.ppermute(value, "ctx", [(0, 1)]))

    pieces_x, pieces_z = {0: x_begun}, {}
    z_far = far(z_in)

    def staged_of(stages):
        inputs = [large[0] if name == "x" else z_far for name, _ in stages]
        shapes = [jax.ShapeDtypeStruct((length, PIECE), BF16) for _ in stages]
        scratch = [pltpu.SemaphoreType.DMA((len(stages),))] if stages else []
        return [piece for _, piece in stages], inputs, shapes, scratch

    def keep(stages, arrays):
        for (name, piece), array in zip(stages, arrays):
            (pieces_x if name == "x" else pieces_z)[piece] = array

    def first(chunk, gate, stages):
        which, inputs, shapes, scratch = staged_of(stages)
        result = pl.pallas_call(
            functools.partial(first_kernel, chunk // in_group, chunk, which),
            in_specs=[scalar] + [near] * 7 + [afar] * len(inputs),
            out_specs=[near] * (1 + len(shapes)),
            out_shape=[hold] + shapes,
            scratch_shapes=scratch,
            compiler_params=pltpu.CompilerParams(vmem_limit_bytes=12 << 20),
            cost_estimate=COST,
            name="first",
        )(place, pieces_x[chunk * CHUNK // PIECE], taps_x, shrink, lines, bc_flat, taps_bc, gate, *inputs)
        keep(stages, result[1:])
        return result[0]

    early = jnp.concatenate([tail[-margin:], bc_near[-margin:].reshape(margin, bc_width)], axis=1)
    ready = first(0, shrink, [])
    early, ready = lax.optimization_barrier((early, ready))
    early = lax.ppermute(early, "ctx", ahead)
    send(ready)
    stages = [("z", 0), ("x", 1)] if last_piece > 0 else [("z", 0)]
    which, inputs, shapes, scratch = staged_of(stages)
    arrays = pl.pallas_call(
        functools.partial(stage_kernel, which),
        out_shape=shapes,
        in_specs=[near] + [afar] * len(inputs),
        out_specs=[near] * len(shapes),
        scratch_shapes=scratch,
        compiler_params=pltpu.CompilerParams(vmem_limit_bytes=8 << 20),
        cost_estimate=COST,
        name="stage",
    )(ready, *inputs)
    keep(stages, arrays)
    stages = [("z", 1)] if last_piece > 0 else []
    which, inputs, shapes, scratch = staged_of(stages)
    left, b_turned, *arrays = pl.pallas_call(
        functools.partial(groups_kernel, groups, which),
        out_shape=[
            jax.ShapeDtypeStruct((groups, length, sub_width), BF16),
            jax.ShapeDtypeStruct((groups, STATE, length), BF16),
        ] + shapes,
        in_specs=[near] * 4 + [afar] * len(inputs),
        out_specs=[near] * (2 + len(shapes)),
        scratch_shapes=scratch or [pltpu.SemaphoreType.DMA((1,))],
        compiler_params=pltpu.CompilerParams(vmem_limit_bytes=12 << 20),
        cost_estimate=COST,
        name="groups",
    )(bc_flat, early, taps_bc, lines, *inputs)
    keep(stages, arrays)

    def local(chunk, gate, stages):
        group, piece = chunk // in_group, chunk * CHUNK // PIECE
        which, inputs, shapes, scratch = staged_of(stages)
        result = pl.pallas_call(
            functools.partial(local_kernel, group, chunk, which),
            in_specs=[near] * 10 + [afar] * len(inputs),
            out_specs=[near] * (4 + len(shapes)),
            out_shape=[
                jax.ShapeDtypeStruct((length, CHUNK), F32),
                jax.ShapeDtypeStruct((length, CHUNK), F32),
                jax.ShapeDtypeStruct((STATE, CHUNK), F32),
                jax.ShapeDtypeStruct((line_rows, CHUNK), F32),
            ] + shapes,
            scratch_shapes=scratch,
            compiler_params=pltpu.CompilerParams(vmem_limit_bytes=LOCAL_VMEM),
            cost_estimate=COST,
            name="local",
        )(
            pieces_x[piece], early, taps_x, pieces_z[piece], left, b_turned, grow, shrink, lines,
            gate, *inputs,
        )
        keep(stages, result[4:])
        return result[:4]

    def combine(owners, chunks, came, gate):
        lanes = [pieces[chunk][3] for chunk in chunks]
        states = [pieces[chunk][2] for chunk in chunks]
        return pl.pallas_call(
            functools.partial(combine_kernel, 2 * subs + 1, owners, len(came)),
            in_specs=[scalar] + [near] * (2 * len(owners) + len(came) + 1),
            out_specs=near,
            out_shape=hold,
            compiler_params=pltpu.CompilerParams(vmem_limit_bytes=8 << 20),
            cost_estimate=COST,
            name="combine",
        )(place, *lanes, *states, *came, gate)

    def absorb(chunk, owners, came, gate):
        group = chunk // in_group
        part, reach = pieces[chunk][:2]
        return pl.pallas_call(
            functools.partial(absorb_kernel, group, owners),
            in_specs=[near] * 3 + [scalar] + [near] * (1 + len(came)),
            out_specs=(near, near),
            out_shape=(
                jax.ShapeDtypeStruct((length, CHUNK), F32),
                jax.ShapeDtypeStruct((length, 128), F32),
            ),
            compiler_params=pltpu.CompilerParams(vmem_limit_bytes=8 << 20),
            cost_estimate=COST,
            name="absorb",
        )(left, part, reach, place, *came, gate)

    def finish(group, done, out, gate):
        rows = SUB
        operands = [gain] + [pair[0] for pair in done] + [pair[1] for pair in done] + [gate]
        specs = [near] * len(operands)
        aliases = {}
        if out is not None:
            aliases = {len(operands): 0}
            operands.append(out)
            specs.append(pl.BlockSpec(memory_space=pl.ANY))
        return pl.pallas_call(
            functools.partial(finish_kernel, group, in_group),
            grid=(length // rows,),
            in_specs=specs,
            out_specs=pl.BlockSpec((rows, per_group), lambda i: (i, group)),
            out_shape=jax.ShapeDtypeStruct((length, channels), BF16),
            input_output_aliases=aliases,
            compiler_params=pltpu.CompilerParams(vmem_limit_bytes=12 << 20),
            cost_estimate=COST,
            name="finish",
        )(*operands)

    pieces, done = {}, []
    gate, out = b_turned, None

    def work(chunk):
        stages = []
        if len(pieces) < last_piece - 1:
            stages = [("x", len(pieces) + 2), ("z", len(pieces) + 2)]
        pieces[chunk] = local(chunk, gate, stages)
        return pieces[chunk][3]

    gate = first(1, gate, [])
    send(gate)
    gate = work(0)
    if count > 2:
        gate = first(2, gate, [])
        send(gate)
    last_step = count - 1 + 2 * max(hops - 2, 0)
    for step in range(last_step + 2):
        senders = [
            owner for owner in range(1, hops) if 0 <= step - 2 * (owner - 1) < count
        ]
        if senders:
            came = [from_first[step]] if step < count else []
            came += [from_later[step - 2]] if step >= 2 else []
            gate = combine(senders, [step - 2 * (owner - 1) for owner in senders], came, gate)
            from_later.append(
                lax.ppermute(gate, "ctx", [(owner, owner + 1) for owner in senders])
            )
        if step + 3 < count:
            gate = first(step + 3, gate, [])
            send(gate)
        if step + 1 < count:
            gate = work(step + 1)
        chunk = step - 1 - 2 * max(hops - 2, 0)
        if 0 <= chunk < count:
            owners = [0] + list(range(2, contexts))
            came = [from_first[chunk]] + [from_later[chunk + 2 * (i - 2)] for i in owners[1:]]
            done.append(absorb(chunk, owners, came, gate))
            gate = done[-1][1]
            if (chunk + 1) % in_group == 0:
                group = chunk // in_group
                out = finish(group, done[group * in_group :], out, gate)
    return out


def solution(mesh):
    placed = (
        P(("groups", "ctx"), ("tp", "fsdp")),
        P(("groups", "ctx"), ("tp", "fsdp"), None),
        P(("groups", "ctx"), ("tp", "fsdp")),
        P(("groups", "ctx"), ("tp", "fsdp")),
        P(None, ("tp", "fsdp")),
        P(None, ("tp", "fsdp"), None),
        P(("tp", "fsdp")),
        P(("tp", "fsdp")),
        P(("tp", "fsdp")),
        P(("tp", "fsdp")),
    )
    return jax.shard_map(
        shards,
        mesh=mesh,
        in_specs=placed,
        out_specs=P(("groups", "ctx"), ("tp", "fsdp")),
        check_vma=False,
    )
```

```python
import functools

import jax
import jax.numpy as jnp
from jax import lax
from jax.experimental import pallas as pl
from jax.experimental.pallas import tpu as pltpu
from jax.sharding import PartitionSpec as P

HEAD_DIM = 64
STATE = 256
KERNEL = 4
SUB = 128
CHUNK = 512
PIECE = 2 * CHUNK
LOCAL_VMEM = 16 << 20
COST = pl.CostEstimate(flops=1 << 10, bytes_accessed=1 << 10, transcendentals=0)
F32 = jnp.float32
BF16 = jnp.bfloat16


def dot(left, right):
    return jnp.dot(left, right, preferred_element_type=F32)


def silu(value):
    half = 0.5 * value
    return half + half * jnp.tanh(half)


def two_terms(value):
    high = value.astype(BF16)
    low = (value - high.astype(F32)).astype(BF16)
    return high, low


def causal_conv(current, earlier, taps):
    length, width = current.shape
    wide = current.astype(F32)
    head = jnp.concatenate([jnp.zeros((8 - KERNEL + 1, width), F32), earlier.astype(F32)], axis=0)
    joined = jnp.concatenate([head, wide], axis=0)
    total = taps[KERNEL - 1 : KERNEL] * wide
    for back in range(1, KERNEL):
        row = KERNEL - 1 - back
        total = total + taps[row : row + 1] * joined[8 - back : 8 - back + length]
    return silu(total).astype(BF16)


def column_of(row):
    size = row.shape[1]
    at = lax.broadcasted_iota(jnp.int32, (size, size), 0)
    of = lax.broadcasted_iota(jnp.int32, (size, size), 1)
    return jnp.sum(jnp.where(at == of, row, 0.0), axis=1, keepdims=True)


def terms_by_row(value):
    high = value.astype(BF16).astype(F32)
    low = value - high
    return jnp.concatenate([high, low], axis=0).T.astype(BF16)


def started(pairs, sems):
    copies = [
        pltpu.make_async_copy(source, target, sems.at[index])
        for index, (source, target) in enumerate(pairs)
    ]
    for copy in copies:
        copy.start()
    return copies


def staging(stages, sources, targets, sems):
    return started(
        [
            (source.at[:, piece * PIECE : (piece + 1) * PIECE], target)
            for piece, source, target in zip(stages, sources, targets)
        ],
        sems,
    )


def steps_kernel(
    x_hbm, taps_x_hbm, taps_bc_hbm, bc_hbm, gain_hbm, dt_hbm, bias_hbm, rate_hbm, skip_hbm,
    x_ref, tail_ref, taps_x_ref, taps_bc_ref, bc_ref, gain_ref, u_ref, v_ref, rows_ref, *scratch
):
    small, (small_sems, whole_sems) = scratch[:4], scratch[4:]
    small_copies = started(zip((dt_hbm, bias_hbm, rate_hbm, skip_hbm), small), small_sems)
    tall, wide = x_ref.shape[0], x_ref.shape[1]
    whole_copies = started(
        (
            (x_hbm.at[tall - 8 : tall, :], tail_ref), (bc_hbm, bc_ref), (taps_bc_hbm, taps_bc_ref),
            (taps_x_hbm, taps_x_ref), (x_hbm.at[:, :wide], x_ref), (gain_hbm, gain_ref),
        ),
        whole_sems,
    )
    for copy in small_copies:
        copy.wait()
    dt_ref, bias_ref, rate_ref, skip_ref = small
    heads, length = dt_ref.shape
    shifted = dt_ref[...].astype(F32) + column_of(bias_ref[...])
    steps = jnp.maximum(shifted, 0.0) + jnp.log1p(jnp.exp(-jnp.abs(shifted)))
    log_decay = -jnp.exp(column_of(rate_ref[...])) * steps
    of = lax.broadcasted_iota(jnp.int32, (length, length), 0)
    at = lax.broadcasted_iota(jnp.int32, (length, length), 1)
    upper = jnp.where(at >= of, 1.0, 0.0).astype(BF16)
    first = log_decay.astype(BF16)
    rest = log_decay - first.astype(F32)
    second = rest.astype(BF16)
    third = (rest - second.astype(F32)).astype(BF16)
    cumulative = dot(first, upper) + dot(second, upper) + dot(third, upper)
    subs = length // SUB
    decays, scales = [], []
    start = jnp.zeros((heads, 1), F32)
    for sub in range(subs):
        rows = slice(sub * SUB, (sub + 1) * SUB)
        inside = cumulative[:, rows] - start
        u_ref[rows, :] = terms_by_row(jnp.exp(inside))
        v_ref[rows, :] = terms_by_row(jnp.exp(-inside) * steps[:, rows])
        end = cumulative[:, (sub + 1) * SUB - 1 : (sub + 1) * SUB]
        decays.append(jnp.exp(end - start))
        scales.append(jnp.exp(start))
        start = end
    lines = decays + scales + [column_of(skip_ref[...]), jnp.exp(start)]
    lane = lax.broadcasted_iota(jnp.int32, (heads, SUB), 1)
    table = jnp.zeros((heads, SUB), F32)
    for index, line in enumerate(lines):
        table = jnp.where(lane == index, line, table)
    rows_ref[...] = terms_by_row(table)[: rows_ref.shape[0]]
    for copy in whole_copies:
        copy.wait()


def stage_kernel(stages, gate_ref, *refs):
    for copy in staging(stages, refs[: len(stages)], refs[len(stages) : -1], refs[-1]):
        copy.wait()


def groups_kernel(groups, stages, bc_ref, early_ref, taps_ref, gate_ref, *refs):
    sources, (left_ref, bt_ref), targets = refs[: len(stages)], refs[len(stages) : len(stages) + 2], refs[len(stages) + 2 : -1]
    copies = staging(stages, sources, targets, refs[-1])
    length = bc_ref.shape[0]
    subs = length // SUB
    of = lax.broadcasted_iota(jnp.int32, (SUB, SUB), 1)
    at = lax.broadcasted_iota(jnp.int32, (SUB, SUB), 0)
    causal = at >= of
    for group in range(groups):
        lanes = slice(group * 2 * STATE, (group + 1) * 2 * STATE)
        base = early_ref.shape[1] - bc_ref.shape[1] + lanes.start
        earlier = early_ref[:, base : base + 2 * STATE]
        conv = causal_conv(bc_ref[:, lanes], earlier, taps_ref[:, group, :])
        b_turned = conv[:, :STATE].astype(F32).T.astype(BF16)
        c_rows = conv[:, STATE:]
        bt_ref[group] = b_turned
        for sub in range(subs):
            rows = slice(sub * SUB, (sub + 1) * SUB)
            scores = jnp.where(causal, dot(c_rows[rows], b_turned[:, rows]), 0.0)
            left_ref[group, rows, :SUB] = scores.astype(BF16)
            left_ref[group, rows, SUB:] = c_rows[rows]
    for copy in copies:
        copy.wait()


def spread_matrix(terms, width, first_head):
    row = lax.broadcasted_iota(jnp.int32, (terms, width), 0)
    lane = lax.broadcasted_iota(jnp.int32, (terms, width), 1)
    heads = terms // 2
    start = (jnp.where(row >= heads, row - heads, row) - first_head) * HEAD_DIM
    return jnp.where((lane >= start) & (lane < start + HEAD_DIM), 1.0, 0.0).astype(BF16)


def next_state(state, scaled, b_turned, decay):
    added = dot(b_turned, scaled)
    return decay * (added if state is None else state + added)


def first_kernel(
    group, chunk, stages, place_ref, x_ref, taps_ref, v_ref, rows_ref, bc_ref, bc_taps_ref, gate_ref, *refs
):
    send_ref = refs[len(stages)]
    copies = staging(stages, refs[: len(stages)], refs[len(stages) + 1 : -1], refs[-1]) if stages else []

    @pl.when(place_ref[0] == 0)
    def _():
        at = slice(chunk * CHUNK, (chunk + 1) * CHUNK)
        length, width = x_ref.shape[0], CHUNK
        spread = spread_matrix(v_ref.shape[1], width, chunk * (CHUNK // HEAD_DIM))
        lanes = dot(rows_ref[...], spread)
        start = group * 2 * STATE
        nothing = jnp.zeros((KERNEL - 1, STATE), BF16)
        b_rows = causal_conv(bc_ref[:, start : start + STATE], nothing, bc_taps_ref[:, group, :STATE])
        b_turned = b_rows.astype(F32).T.astype(BF16)
        nothing = jnp.zeros((KERNEL - 1, width), BF16)
        inner_at = slice(chunk * CHUNK % PIECE, chunk * CHUNK % PIECE + CHUNK)
        conv = causal_conv(x_ref[:, inner_at], nothing, taps_ref[:, at])
        state = None
        for sub in range(length // SUB):
            rows = slice(sub * SUB, (sub + 1) * SUB)
            scaled = (conv[rows].astype(F32) * dot(v_ref[rows], spread)).astype(BF16)
            state = next_state(state, scaled, b_turned[:, rows], lanes[sub : sub + 1])
        send_ref[...] = state.astype(send_ref.dtype)

    for copy in copies:
        copy.wait()


def local_kernel(
    group, chunk, stages, x_ref, early_ref, taps_ref, z_ref, left_ref, bt_ref, u_ref, v_ref, rows_ref,
    gate_ref, *refs
):
    outs = len(stages)
    part_ref, reach_ref, state_ref, lanes_ref = refs[outs : outs + 4]
    copies = staging(stages, refs[:outs], refs[outs + 4 : -1], refs[-1]) if stages else []
    lanes_at = slice(chunk * CHUNK, (chunk + 1) * CHUNK)
    inner_at = slice(chunk * CHUNK % PIECE, chunk * CHUNK % PIECE + CHUNK)
    length, width = x_ref.shape[0], CHUNK
    spread = spread_matrix(u_ref.shape[1], width, chunk * (CHUNK // HEAD_DIM))
    lanes = dot(rows_ref[...], spread)
    lanes_ref[...] = lanes
    conv = causal_conv(x_ref[:, inner_at], early_ref[:, lanes_at], taps_ref[:, lanes_at])
    subs = length // SUB
    skip = lanes[2 * subs : 2 * subs + 1]
    state = None
    for sub in range(subs):
        rows = slice(sub * SUB, (sub + 1) * SUB)
        inputs = conv[rows].astype(F32)
        scaled = (inputs * dot(v_ref[rows], spread)).astype(BF16)
        inner = dot(left_ref[group, rows, :SUB], scaled)
        if sub > 0:
            inner = inner + dot(left_ref[group, rows, SUB:], state.astype(BF16))
        state = next_state(state, scaled, bt_ref[group, :, rows], lanes[sub : sub + 1])
        grown = dot(u_ref[rows], spread)
        gate = silu(z_ref[rows, inner_at].astype(F32))
        part_ref[rows, :] = gate * (grown * inner + skip * inputs)
        reach_ref[rows, :] = gate * grown * lanes[subs + sub : subs + sub + 1]
    state_ref[...] = state
    for copy in copies:
        copy.wait()


def combine_kernel(line, owners, arrivals, place_ref, *refs):
    place = place_ref[0]
    lanes = refs[: len(owners)]
    states = refs[len(owners) : 2 * len(owners)]
    came = refs[2 * len(owners) : 2 * len(owners) + arrivals]
    sent_ref = refs[-1]
    total, state = lanes[0][line : line + 1], states[0][...]
    for owner, lane_ref, state_ref in zip(owners[1:], lanes[1:], states[1:]):
        total = jnp.where(place >= owner, lane_ref[line : line + 1], total)
        state = jnp.where(place >= owner, state_ref[...], state)
    value = came[0][...].astype(F32)
    for other in came[1:]:
        value = jnp.where(place >= 2, other[...].astype(F32), value)
    sent_ref[...] = (total * value + state).astype(sent_ref.dtype)


def arrived_state(place, owners, refs):
    incoming = refs[0][...].astype(F32)
    for owner, other in zip(owners[1:], refs[1:]):
        incoming = jnp.where(place >= owner, other[...].astype(F32), incoming)
    return incoming.astype(BF16)


def absorb_kernel(group, chunk, owners, place_ref, left_ref, gain_ref, part_ref, reach_ref, *refs):
    length, width = part_ref.shape
    gated_ref, square_ref = refs[-2:]
    incoming = arrived_state(place_ref[0], owners, refs[: len(owners)])
    gain = gain_ref[:, chunk * CHUNK : (chunk + 1) * CHUNK]
    for start in range(0, length, SUB):
        rows = slice(start, start + SUB)
        value = part_ref[rows] + reach_ref[rows] * dot(left_ref[group, rows, SUB:], incoming)
        gated_ref[rows, :] = value * gain
        power = value * value
        total = power[:, :128]
        for lane in range(128, width, 128):
            total = total + power[:, lane : lane + 128]
        square_ref[rows, :] = total


def finish_kernel(group, chunks, owners, place_ref, left_ref, gain_ref, part_ref, reach_ref, *refs):
    length, width = part_ref.shape
    came, refs = refs[: len(owners)], refs[len(owners) :]
    gated, squares = refs[: chunks - 1], refs[chunks - 1 : 2 * chunks - 2]
    out_hbm, out_ref, sems = refs[-3:]
    incoming = arrived_state(place_ref[0], owners, came)
    first_lane = group * chunks * width
    last = slice(first_lane + (chunks - 1) * width, first_lane + chunks * width)
    copies = []
    for start in range(0, length, SUB):
        rows = slice(start, start + SUB)
        value = part_ref[rows] + reach_ref[rows] * dot(left_ref[group, rows, SUB:], incoming)
        square = jnp.sum(value * value, axis=1, keepdims=True)
        if chunks > 1:
            total = squares[0][rows]
            for other in squares[1:]:
                total = total + other[rows]
            square = square + jnp.sum(total, axis=1, keepdims=True)
        scale = lax.rsqrt(square * (1.0 / (width * chunks)) + 1e-05)
        for index in range(chunks):
            scaled = value * gain_ref[:, last] if index == chunks - 1 else gated[index][rows]
            lanes = slice(index * width, (index + 1) * width)
            out_ref[rows, lanes] = (scaled * scale).astype(BF16)
            copies.append(
                pltpu.make_async_copy(
                    out_ref.at[rows, lanes],
                    out_hbm.at[rows, first_lane + index * width : first_lane + (index + 1) * width],
                    sems.at[len(copies)],
                )
            )
            copies[-1].start()
    for copy in copies:
        copy.wait()


def shards(x_in, bc_in, z_in, dt_in, conv_x, conv_bc, dt_bias, a_log, d_skip, norm_gain):
    length, channels = x_in.shape
    groups = bc_in.shape[1]
    heads = channels // HEAD_DIM
    contexts = lax.axis_size("ctx")
    wire = BF16 if contexts <= 8 else F32
    margin = KERNEL - 1
    subs = length // SUB
    ahead = [(i, i + 1) for i in range(contexts - 1)]
    bc_width = groups * 2 * STATE
    line_rows = -(-(2 * subs + 2) // 8) * 8
    sub_width = SUB + STATE
    place = lax.axis_index("ctx").astype(jnp.int32).reshape(1)
    small = (dt_in.T, dt_bias.reshape(1, heads), a_log.reshape(1, heads), d_skip.reshape(1, heads))
    far = lambda array: pltpu.with_memory_space_constraint(array, pltpu.HBM)
    large = tuple(far(array) for array in (x_in, conv_x, conv_bc, bc_in, norm_gain.reshape(1, channels)))
    begun = PIECE
    x_begun, tail, taps_x, taps_bc, bc_near, gain, grow, shrink, lines = pl.pallas_call(
        steps_kernel,
        in_specs=[pl.BlockSpec(memory_space=pltpu.HBM)] * (len(large) + len(small)),
        out_specs=[pl.BlockSpec(memory_space=pltpu.VMEM)] * 9,
        out_shape=(
            jax.ShapeDtypeStruct((length, begun), BF16),
            jax.ShapeDtypeStruct((8, channels), BF16),
            jax.ShapeDtypeStruct(conv_x.shape, F32),
            jax.ShapeDtypeStruct(conv_bc.shape, F32),
            jax.ShapeDtypeStruct(bc_in.shape, BF16),
            jax.ShapeDtypeStruct((1, channels), F32),
            jax.ShapeDtypeStruct((length, 2 * heads), BF16),
            jax.ShapeDtypeStruct((length, 2 * heads), BF16),
            jax.ShapeDtypeStruct((line_rows, 2 * heads), BF16),
        ),
        scratch_shapes=[pltpu.VMEM(array.shape, array.dtype) for array in small] + [
            pltpu.SemaphoreType.DMA((len(small),)), pltpu.SemaphoreType.DMA((6,)),
        ],
        compiler_params=pltpu.CompilerParams(vmem_limit_bytes=12 << 20),
        cost_estimate=COST,
        name="steps",
    )(*large, *[far(array) for array in small])
    bc_flat = bc_near.reshape(length, bc_width)
    per_group = channels // groups
    in_group = per_group // CHUNK
    count = channels // CHUNK
    hops = contexts - 1
    near = pl.BlockSpec(memory_space=pltpu.VMEM)
    scalar = pl.BlockSpec(memory_space=pltpu.SMEM)
    afar = pl.BlockSpec(memory_space=pltpu.HBM)
    last_piece = channels // PIECE - 1
    hold = jax.ShapeDtypeStruct((STATE, CHUNK), wire)
    from_first, from_later = [], []

    def send(value):
        from_first.append(lax.ppermute(value, "ctx", [(0, 1)]))

    pieces_x, pieces_z = {0: x_begun}, {}
    z_far = far(z_in)

    def staged_of(stages):
        inputs = [large[0] if name == "x" else z_far for name, _ in stages]
        shapes = [jax.ShapeDtypeStruct((length, PIECE), BF16) for _ in stages]
        scratch = [pltpu.SemaphoreType.DMA((len(stages),))] if stages else []
        return [piece for _, piece in stages], inputs, shapes, scratch

    def keep(stages, arrays):
        for (name, piece), array in zip(stages, arrays):
            (pieces_x if name == "x" else pieces_z)[piece] = array

    def first(chunk, gate, stages):
        which, inputs, shapes, scratch = staged_of(stages)
        result = pl.pallas_call(
            functools.partial(first_kernel, chunk // in_group, chunk, which),
            in_specs=[scalar] + [near] * 7 + [afar] * len(inputs),
            out_specs=[near] * (1 + len(shapes)),
            out_shape=[hold] + shapes,
            scratch_shapes=scratch,
            compiler_params=pltpu.CompilerParams(vmem_limit_bytes=12 << 20),
            cost_estimate=COST,
            name="first",
        )(place, pieces_x[chunk * CHUNK // PIECE], taps_x, shrink, lines, bc_flat, taps_bc, gate, *inputs)
        keep(stages, result[1:])
        return result[0]

    early = jnp.concatenate([tail[-margin:], bc_near[-margin:].reshape(margin, bc_width)], axis=1)
    ready = first(0, shrink, [])
    early, ready = lax.optimization_barrier((early, ready))
    early = lax.ppermute(early, "ctx", ahead)
    send(ready)
    stages = [("z", 0), ("x", 1)] if last_piece > 0 else [("z", 0)]
    which, inputs, shapes, scratch = staged_of(stages)
    arrays = pl.pallas_call(
        functools.partial(stage_kernel, which),
        out_shape=shapes,
        in_specs=[near] + [afar] * len(inputs),
        out_specs=[near] * len(shapes),
        scratch_shapes=scratch,
        compiler_params=pltpu.CompilerParams(vmem_limit_bytes=8 << 20),
        cost_estimate=COST,
        name="stage",
    )(ready, *inputs)
    keep(stages, arrays)
    stages = [("z", 1)] if last_piece > 0 else []
    which, inputs, shapes, scratch = staged_of(stages)
    left, b_turned, *arrays = pl.pallas_call(
        functools.partial(groups_kernel, groups, which),
        out_shape=[
            jax.ShapeDtypeStruct((groups, length, sub_width), BF16),
            jax.ShapeDtypeStruct((groups, STATE, length), BF16),
        ] + shapes,
        in_specs=[near] * 4 + [afar] * len(inputs),
        out_specs=[near] * (2 + len(shapes)),
        scratch_shapes=scratch or [pltpu.SemaphoreType.DMA((1,))],
        compiler_params=pltpu.CompilerParams(vmem_limit_bytes=12 << 20),
        cost_estimate=COST,
        name="groups",
    )(bc_flat, early, taps_bc, lines, *inputs)
    keep(stages, arrays)

    def local(chunk, gate, stages):
        group, piece = chunk // in_group, chunk * CHUNK // PIECE
        which, inputs, shapes, scratch = staged_of(stages)
        result = pl.pallas_call(
            functools.partial(local_kernel, group, chunk, which),
            in_specs=[near] * 10 + [afar] * len(inputs),
            out_specs=[near] * (4 + len(shapes)),
            out_shape=[
                jax.ShapeDtypeStruct((length, CHUNK), F32),
                jax.ShapeDtypeStruct((length, CHUNK), F32),
                jax.ShapeDtypeStruct((STATE, CHUNK), F32),
                jax.ShapeDtypeStruct((line_rows, CHUNK), F32),
            ] + shapes,
            scratch_shapes=scratch,
            compiler_params=pltpu.CompilerParams(vmem_limit_bytes=LOCAL_VMEM),
            cost_estimate=COST,
            name="local",
        )(
            pieces_x[piece], early, taps_x, pieces_z[piece], left, b_turned, grow, shrink, lines,
            gate, *inputs,
        )
        keep(stages, result[4:])
        return result[:4]

    def combine(owners, chunks, came, gate):
        lanes = [pieces[chunk][3] for chunk in chunks]
        states = [pieces[chunk][2] for chunk in chunks]
        return pl.pallas_call(
            functools.partial(combine_kernel, 2 * subs + 1, owners, len(came)),
            in_specs=[scalar] + [near] * (2 * len(owners) + len(came) + 1),
            out_specs=near,
            out_shape=hold,
            compiler_params=pltpu.CompilerParams(vmem_limit_bytes=8 << 20),
            cost_estimate=COST,
            name="combine",
        )(place, *lanes, *states, *came, gate)

    def absorb(chunk, owners, came, gate):
        part, reach = pieces[chunk][:2]
        return pl.pallas_call(
            functools.partial(absorb_kernel, chunk // in_group, chunk, owners),
            in_specs=[scalar] + [near] * (5 + len(came)),
            out_specs=(near, near),
            out_shape=(
                jax.ShapeDtypeStruct((length, CHUNK), F32),
                jax.ShapeDtypeStruct((length, 128), F32),
            ),
            compiler_params=pltpu.CompilerParams(vmem_limit_bytes=8 << 20),
            cost_estimate=COST,
            name="absorb",
        )(place, left, gain, part, reach, *came, gate)

    def finish(chunk, owners, came, done, out, gate):
        part, reach = pieces[chunk][:2]
        operands = [place, left, gain, part, reach, *came]
        operands += [pair[0] for pair in done] + [pair[1] for pair in done] + [gate]
        specs = [scalar] + [near] * (len(operands) - 1)
        aliases = {}
        if out is not None:
            aliases = {len(operands): 0}
            operands.append(far(out))
            specs.append(afar)
        return pl.pallas_call(
            functools.partial(finish_kernel, chunk // in_group, in_group, owners),
            in_specs=specs,
            out_specs=afar,
            out_shape=jax.ShapeDtypeStruct((length, channels), BF16),
            input_output_aliases=aliases,
            scratch_shapes=[
                pltpu.VMEM((length, per_group), BF16),
                pltpu.SemaphoreType.DMA((length // SUB * in_group,)),
            ],
            compiler_params=pltpu.CompilerParams(vmem_limit_bytes=12 << 20),
            cost_estimate=COST,
            name="finish",
        )(*operands)

    pieces, done = {}, []
    gate, out = b_turned, None

    def work(chunk):
        stages = []
        if len(pieces) < last_piece - 1:
            stages = [("x", len(pieces) + 2), ("z", len(pieces) + 2)]
        pieces[chunk] = local(chunk, gate, stages)
        return pieces[chunk][3]

    gate = first(1, gate, [])
    send(gate)
    gate = work(0)
    if count > 2:
        gate = first(2, gate, [])
        send(gate)
    last_step = count - 1 + 2 * max(hops - 2, 0)
    for step in range(last_step + 2):
        senders = [
            owner for owner in range(1, hops) if 0 <= step - 2 * (owner - 1) < count
        ]
        if senders:
            came = [from_first[step]] if step < count else []
            came += [from_later[step - 2]] if step >= 2 else []
            gate = combine(senders, [step - 2 * (owner - 1) for owner in senders], came, gate)
            from_later.append(
                lax.ppermute(gate, "ctx", [(owner, owner + 1) for owner in senders])
            )
        if step + 3 < count:
            gate = first(step + 3, gate, [])
            send(gate)
        if step + 1 < count:
            gate = work(step + 1)
        chunk = step - 1 - 2 * max(hops - 2, 0)
        if 0 <= chunk < count:
            owners = [0] + list(range(2, contexts))
            came = [from_first[chunk]] + [from_later[chunk + 2 * (i - 2)] for i in owners[1:]]
            if (chunk + 1) % in_group:
                done.append(absorb(chunk, owners, came, gate))
                gate = done[-1][1]
            else:
                out = finish(chunk, owners, came, done, out, gate)
                done = []
    return out


def solution(mesh):
    placed = (
        P(("groups", "ctx"), ("tp", "fsdp")),
        P(("groups", "ctx"), ("tp", "fsdp"), None),
        P(("groups", "ctx"), ("tp", "fsdp")),
        P(("groups", "ctx"), ("tp", "fsdp")),
        P(None, ("tp", "fsdp")),
        P(None, ("tp", "fsdp"), None),
        P(("tp", "fsdp")),
        P(("tp", "fsdp")),
        P(("tp", "fsdp")),
        P(("tp", "fsdp")),
    )
    return jax.shard_map(
        shards,
        mesh=mesh,
        in_specs=placed,
        out_specs=P(("groups", "ctx"), ("tp", "fsdp")),
        check_vma=False,
    )
```

```python
import functools

import jax
import jax.numpy as jnp
from jax import lax
from jax.experimental import pallas as pl
from jax.experimental.pallas import tpu as pltpu
from jax.sharding import PartitionSpec as P

HEAD_DIM = 64
STATE = 256
KERNEL = 4
SUB = 128
CHUNK = 512
PIECE = 2 * CHUNK
LOCAL_VMEM = 16 << 20
COST = pl.CostEstimate(flops=1 << 10, bytes_accessed=1 << 10, transcendentals=0)
F32 = jnp.float32
BF16 = jnp.bfloat16


def dot(left, right):
    return jnp.dot(left, right, preferred_element_type=F32)


def silu(value):
    half = 0.5 * value
    return half + half * jnp.tanh(half)


def two_terms(value):
    high = value.astype(BF16)
    low = (value - high.astype(F32)).astype(BF16)
    return high, low


def causal_conv(current, earlier, taps):
    length, width = current.shape
    wide = current.astype(F32)
    head = jnp.concatenate([jnp.zeros((8 - KERNEL + 1, width), F32), earlier.astype(F32)], axis=0)
    joined = jnp.concatenate([head, wide], axis=0)
    total = taps[KERNEL - 1 : KERNEL] * wide
    for back in range(1, KERNEL):
        row = KERNEL - 1 - back
        total = total + taps[row : row + 1] * joined[8 - back : 8 - back + length]
    return silu(total).astype(BF16)


def column_of(row):
    size = row.shape[1]
    at = lax.broadcasted_iota(jnp.int32, (size, size), 0)
    of = lax.broadcasted_iota(jnp.int32, (size, size), 1)
    return jnp.sum(jnp.where(at == of, row, 0.0), axis=1, keepdims=True)


def terms_by_row(value):
    high = value.astype(BF16).astype(F32)
    low = value - high
    return jnp.concatenate([high, low], axis=0).T.astype(BF16)


def started(pairs, sems):
    copies = [
        pltpu.make_async_copy(source, target, sems.at[index])
        for index, (source, target) in enumerate(pairs)
    ]
    for copy in copies:
        copy.start()
    return copies


def staging(stages, sources, targets, sems):
    return started(
        [
            (source.at[:, piece * PIECE : (piece + 1) * PIECE], target)
            for piece, source, target in zip(stages, sources, targets)
        ],
        sems,
    )


def steps_kernel(
    x_hbm, taps_x_hbm, taps_bc_hbm, bc_hbm, gain_hbm, dt_hbm, bias_hbm, rate_hbm, skip_hbm,
    x_ref, tail_ref, taps_x_ref, taps_bc_ref, bc_ref, gain_ref, u_ref, v_ref, rows_ref, *scratch
):
    small, (small_sems, whole_sems) = scratch[:4], scratch[4:]
    small_copies = started(zip((dt_hbm, bias_hbm, rate_hbm, skip_hbm), small), small_sems)
    tall, wide = x_ref.shape[0], x_ref.shape[1]
    whole_copies = started(
        (
            (x_hbm.at[tall - 8 : tall, :], tail_ref), (bc_hbm, bc_ref), (taps_bc_hbm, taps_bc_ref),
            (taps_x_hbm, taps_x_ref), (x_hbm.at[:, :wide], x_ref), (gain_hbm, gain_ref),
        ),
        whole_sems,
    )
    for copy in small_copies:
        copy.wait()
    dt_ref, bias_ref, rate_ref, skip_ref = small
    heads, length = dt_ref.shape
    shifted = dt_ref[...].astype(F32) + column_of(bias_ref[...])
    steps = jnp.maximum(shifted, 0.0) + jnp.log1p(jnp.exp(-jnp.abs(shifted)))
    log_decay = -jnp.exp(column_of(rate_ref[...])) * steps
    of = lax.broadcasted_iota(jnp.int32, (length, length), 0)
    at = lax.broadcasted_iota(jnp.int32, (length, length), 1)
    upper = jnp.where(at >= of, 1.0, 0.0).astype(BF16)
    first = log_decay.astype(BF16)
    rest = log_decay - first.astype(F32)
    second = rest.astype(BF16)
    third = (rest - second.astype(F32)).astype(BF16)
    cumulative = dot(first, upper) + dot(second, upper) + dot(third, upper)
    subs = length // SUB
    decays, scales = [], []
    start = jnp.zeros((heads, 1), F32)
    for sub in range(subs):
        rows = slice(sub * SUB, (sub + 1) * SUB)
        inside = cumulative[:, rows] - start
        u_ref[rows, :] = terms_by_row(jnp.exp(inside))
        v_ref[rows, :] = terms_by_row(jnp.exp(-inside) * steps[:, rows])
        end = cumulative[:, (sub + 1) * SUB - 1 : (sub + 1) * SUB]
        decays.append(jnp.exp(end - start))
        scales.append(jnp.exp(start))
        start = end
    lines = decays + scales + [column_of(skip_ref[...]), jnp.exp(start)]
    lane = lax.broadcasted_iota(jnp.int32, (heads, SUB), 1)
    table = jnp.zeros((heads, SUB), F32)
    for index, line in enumerate(lines):
        table = jnp.where(lane == index, line, table)
    rows_ref[...] = terms_by_row(table)[: rows_ref.shape[0]]
    for copy in whole_copies:
        copy.wait()


def stage_kernel(stages, gate_ref, *refs):
    for copy in staging(stages, refs[: len(stages)], refs[len(stages) : -1], refs[-1]):
        copy.wait()


def groups_kernel(groups, stages, bc_ref, early_ref, taps_ref, gate_ref, *refs):
    sources, (left_ref, bt_ref), targets = refs[: len(stages)], refs[len(stages) : len(stages) + 2], refs[len(stages) + 2 : -1]
    copies = staging(stages, sources, targets, refs[-1])
    length = bc_ref.shape[0]
    subs = length // SUB
    of = lax.broadcasted_iota(jnp.int32, (SUB, SUB), 1)
    at = lax.broadcasted_iota(jnp.int32, (SUB, SUB), 0)
    causal = at >= of
    for group in range(groups):
        lanes = slice(group * 2 * STATE, (group + 1) * 2 * STATE)
        base = early_ref.shape[1] - bc_ref.shape[1] + lanes.start
        earlier = early_ref[:, base : base + 2 * STATE]
        conv = causal_conv(bc_ref[:, lanes], earlier, taps_ref[:, group, :])
        b_turned = conv[:, :STATE].astype(F32).T.astype(BF16)
        c_rows = conv[:, STATE:]
        bt_ref[group] = b_turned
        for sub in range(subs):
            rows = slice(sub * SUB, (sub + 1) * SUB)
            scores = jnp.where(causal, dot(c_rows[rows], b_turned[:, rows]), 0.0)
            left_ref[group, rows, :SUB] = scores.astype(BF16)
            left_ref[group, rows, SUB:] = c_rows[rows]
    for copy in copies:
        copy.wait()


def spread_matrix(terms, width, first_head):
    row = lax.broadcasted_iota(jnp.int32, (terms, width), 0)
    lane = lax.broadcasted_iota(jnp.int32, (terms, width), 1)
    heads = terms // 2
    start = (jnp.where(row >= heads, row - heads, row) - first_head) * HEAD_DIM
    return jnp.where((lane >= start) & (lane < start + HEAD_DIM), 1.0, 0.0).astype(BF16)


def next_state(state, scaled, b_turned, decay):
    added = dot(b_turned, scaled)
    return decay * (added if state is None else state + added)


def first_kernel(
    group, chunk, stages, place_ref, x_ref, taps_ref, v_ref, rows_ref, bc_ref, bc_taps_ref, gate_ref, *refs
):
    send_ref = refs[len(stages)]
    copies = staging(stages, refs[: len(stages)], refs[len(stages) + 1 : -1], refs[-1]) if stages else []

    @pl.when(place_ref[0] == 0)
    def _():
        at = slice(chunk * CHUNK, (chunk + 1) * CHUNK)
        length, width = x_ref.shape[0], CHUNK
        spread = spread_matrix(v_ref.shape[1], width, chunk * (CHUNK // HEAD_DIM))
        lanes = dot(rows_ref[...], spread)
        start = group * 2 * STATE
        nothing = jnp.zeros((KERNEL - 1, STATE), BF16)
        b_rows = causal_conv(bc_ref[:, start : start + STATE], nothing, bc_taps_ref[:, group, :STATE])
        b_turned = b_rows.astype(F32).T.astype(BF16)
        nothing = jnp.zeros((KERNEL - 1, width), BF16)
        inner_at = slice(chunk * CHUNK % PIECE, chunk * CHUNK % PIECE + CHUNK)
        conv = causal_conv(x_ref[:, inner_at], nothing, taps_ref[:, at])
        state = None
        for sub in range(length // SUB):
            rows = slice(sub * SUB, (sub + 1) * SUB)
            scaled = (conv[rows].astype(F32) * dot(v_ref[rows], spread)).astype(BF16)
            state = next_state(state, scaled, b_turned[:, rows], lanes[sub : sub + 1])
        send_ref[...] = state.astype(send_ref.dtype)

    for copy in copies:
        copy.wait()


def local_kernel(
    group, chunk, stages, x_ref, early_ref, taps_ref, z_ref, left_ref, bt_ref, u_ref, v_ref, rows_ref,
    gate_ref, *refs
):
    outs = len(stages)
    part_ref, reach_ref, state_ref, lanes_ref = refs[outs : outs + 4]
    copies = staging(stages, refs[:outs], refs[outs + 4 : -1], refs[-1]) if stages else []
    lanes_at = slice(chunk * CHUNK, (chunk + 1) * CHUNK)
    inner_at = slice(chunk * CHUNK % PIECE, chunk * CHUNK % PIECE + CHUNK)
    length, width = x_ref.shape[0], CHUNK
    spread = spread_matrix(u_ref.shape[1], width, chunk * (CHUNK // HEAD_DIM))
    lanes = dot(rows_ref[...], spread)
    lanes_ref[...] = lanes
    conv = causal_conv(x_ref[:, inner_at], early_ref[:, lanes_at], taps_ref[:, lanes_at])
    subs = length // SUB
    skip = lanes[2 * subs : 2 * subs + 1]
    state = None
    for sub in range(subs):
        rows = slice(sub * SUB, (sub + 1) * SUB)
        inputs = conv[rows].astype(F32)
        scaled = (inputs * dot(v_ref[rows], spread)).astype(BF16)
        inner = dot(left_ref[group, rows, :SUB], scaled)
        if sub > 0:
            inner = inner + dot(left_ref[group, rows, SUB:], state.astype(BF16))
        state = next_state(state, scaled, bt_ref[group, :, rows], lanes[sub : sub + 1])
        grown = dot(u_ref[rows], spread)
        gate = silu(z_ref[rows, inner_at].astype(F32))
        part_ref[rows, :] = gate * (grown * inner + skip * inputs)
        reach_ref[rows, :] = gate * grown * lanes[subs + sub : subs + sub + 1]
    state_ref[...] = state
    for copy in copies:
        copy.wait()


def combine_kernel(line, owners, arrivals, place_ref, *refs):
    place = place_ref[0]
    lanes = refs[: len(owners)]
    states = refs[len(owners) : 2 * len(owners)]
    came = refs[2 * len(owners) : 2 * len(owners) + arrivals]
    sent_ref = refs[-1]
    total, state = lanes[0][line : line + 1], states[0][...]
    for owner, lane_ref, state_ref in zip(owners[1:], lanes[1:], states[1:]):
        total = jnp.where(place >= owner, lane_ref[line : line + 1], total)
        state = jnp.where(place >= owner, state_ref[...], state)
    value = came[0][...].astype(F32)
    for other in came[1:]:
        value = jnp.where(place >= 2, other[...].astype(F32), value)
    sent_ref[...] = (total * value + state).astype(sent_ref.dtype)


def arrived_state(place, owners, refs):
    incoming = refs[0][...].astype(F32)
    for owner, other in zip(owners[1:], refs[1:]):
        incoming = jnp.where(place >= owner, other[...].astype(F32), incoming)
    return incoming.astype(BF16)


def absorb_kernel(group, chunk, owners, place_ref, left_ref, gain_ref, part_ref, reach_ref, *refs):
    length, width = part_ref.shape
    gated_ref, square_ref = refs[-2:]
    incoming = arrived_state(place_ref[0], owners, refs[: len(owners)])
    gain = gain_ref[:, chunk * CHUNK : (chunk + 1) * CHUNK]
    for start in range(0, length, SUB):
        rows = slice(start, start + SUB)
        value = part_ref[rows] + reach_ref[rows] * dot(left_ref[group, rows, SUB:], incoming)
        gated_ref[rows, :] = value * gain
        power = value * value
        total = power[:, :128]
        for lane in range(128, width, 128):
            total = total + power[:, lane : lane + 128]
        square_ref[rows, :] = total


def finish_kernel(group, chunks, owners, place_ref, left_ref, gain_ref, part_ref, reach_ref, *refs):
    length, width = part_ref.shape
    came, refs = refs[: len(owners)], refs[len(owners) :]
    gated, squares = refs[: chunks - 1], refs[chunks - 1 : 2 * chunks - 2]
    out_hbm, out_ref, sems = refs[-3:]
    incoming = arrived_state(place_ref[0], owners, came)
    first_lane = group * chunks * width
    last = slice(first_lane + (chunks - 1) * width, first_lane + chunks * width)
    copies = []
    for start in range(0, length, SUB):
        rows = slice(start, start + SUB)
        value = part_ref[rows] + reach_ref[rows] * dot(left_ref[group, rows, SUB:], incoming)
        square = jnp.sum(value * value, axis=1, keepdims=True)
        if chunks > 1:
            total = squares[0][rows]
            for other in squares[1:]:
                total = total + other[rows]
            square = square + jnp.sum(total, axis=1, keepdims=True)
        scale = lax.rsqrt(square * (1.0 / (width * chunks)) + 1e-05)
        for index in range(chunks):
            scaled = value * gain_ref[:, last] if index == chunks - 1 else gated[index][rows]
            lanes = slice(index * width, (index + 1) * width)
            out_ref[rows, lanes] = (scaled * scale).astype(BF16)
            copies.append(
                pltpu.make_async_copy(
                    out_ref.at[rows, lanes],
                    out_hbm.at[rows, first_lane + index * width : first_lane + (index + 1) * width],
                    sems.at[len(copies)],
                )
            )
            copies[-1].start()
    for copy in copies:
        copy.wait()


def shards(x_in, bc_in, z_in, dt_in, conv_x, conv_bc, dt_bias, a_log, d_skip, norm_gain):
    length, channels = x_in.shape
    groups = bc_in.shape[1]
    heads = channels // HEAD_DIM
    contexts = lax.axis_size("ctx")
    wire = BF16 if contexts <= 8 else F32
    margin = KERNEL - 1
    subs = length // SUB
    ahead = [(i, i + 1) for i in range(contexts - 1)]
    bc_width = groups * 2 * STATE
    line_rows = -(-(2 * subs + 2) // 8) * 8
    sub_width = SUB + STATE
    place = lax.axis_index("ctx").astype(jnp.int32).reshape(1)
    small = (dt_in.T, dt_bias.reshape(1, heads), a_log.reshape(1, heads), d_skip.reshape(1, heads))
    far = lambda array: pltpu.with_memory_space_constraint(array, pltpu.HBM)
    large = tuple(far(array) for array in (x_in, conv_x, conv_bc, bc_in, norm_gain.reshape(1, channels)))
    begun = PIECE
    x_begun, tail, taps_x, taps_bc, bc_near, gain, grow, shrink, lines = pl.pallas_call(
        steps_kernel,
        in_specs=[pl.BlockSpec(memory_space=pltpu.HBM)] * (len(large) + len(small)),
        out_specs=[pl.BlockSpec(memory_space=pltpu.VMEM)] * 9,
        out_shape=(
            jax.ShapeDtypeStruct((length, begun), BF16),
            jax.ShapeDtypeStruct((8, channels), BF16),
            jax.ShapeDtypeStruct(conv_x.shape, F32),
            jax.ShapeDtypeStruct(conv_bc.shape, F32),
            jax.ShapeDtypeStruct(bc_in.shape, BF16),
            jax.ShapeDtypeStruct((1, channels), F32),
            jax.ShapeDtypeStruct((length, 2 * heads), BF16),
            jax.ShapeDtypeStruct((length, 2 * heads), BF16),
            jax.ShapeDtypeStruct((line_rows, 2 * heads), BF16),
        ),
        scratch_shapes=[pltpu.VMEM(array.shape, array.dtype) for array in small] + [
            pltpu.SemaphoreType.DMA((len(small),)), pltpu.SemaphoreType.DMA((6,)),
        ],
        compiler_params=pltpu.CompilerParams(vmem_limit_bytes=12 << 20),
        cost_estimate=COST,
        name="steps",
    )(*large, *[far(array) for array in small])
    bc_flat = bc_near.reshape(length, bc_width)
    per_group = channels // groups
    in_group = per_group // CHUNK
    count = channels // CHUNK
    hops = contexts - 1
    near = pl.BlockSpec(memory_space=pltpu.VMEM)
    scalar = pl.BlockSpec(memory_space=pltpu.SMEM)
    afar = pl.BlockSpec(memory_space=pltpu.HBM)
    last_piece = channels // PIECE - 1
    hold = jax.ShapeDtypeStruct((STATE, CHUNK), wire)
    from_first, from_later = [], []

    def send(value):
        from_first.append(lax.ppermute(value, "ctx", [(0, 1)]))

    pieces_x, pieces_z = {0: x_begun}, {}
    z_far = far(z_in)

    def staged_of(stages):
        inputs = [large[0] if name == "x" else z_far for name, _ in stages]
        shapes = [jax.ShapeDtypeStruct((length, PIECE), BF16) for _ in stages]
        scratch = [pltpu.SemaphoreType.DMA((len(stages),))] if stages else []
        return [piece for _, piece in stages], inputs, shapes, scratch

    def keep(stages, arrays):
        for (name, piece), array in zip(stages, arrays):
            (pieces_x if name == "x" else pieces_z)[piece] = array

    def first(chunk, gate, stages):
        which, inputs, shapes, scratch = staged_of(stages)
        result = pl.pallas_call(
            functools.partial(first_kernel, chunk // in_group, chunk, which),
            in_specs=[scalar] + [near] * 7 + [afar] * len(inputs),
            out_specs=[near] * (1 + len(shapes)),
            out_shape=[hold] + shapes,
            scratch_shapes=scratch,
            compiler_params=pltpu.CompilerParams(vmem_limit_bytes=12 << 20),
            cost_estimate=COST,
            name="first",
        )(place, pieces_x[chunk * CHUNK // PIECE], taps_x, shrink, lines, bc_flat, taps_bc, gate, *inputs)
        keep(stages, result[1:])
        return result[0]

    early = jnp.concatenate([tail[-margin:], bc_near[-margin:].reshape(margin, bc_width)], axis=1)
    ready = first(0, shrink, [])
    early, ready = lax.optimization_barrier((early, ready))
    early = lax.ppermute(early, "ctx", ahead)
    send(ready)
    stages = [("z", 0), ("x", 1)] if last_piece > 0 else [("z", 0)]
    which, inputs, shapes, scratch = staged_of(stages)
    arrays = pl.pallas_call(
        functools.partial(stage_kernel, which),
        out_shape=shapes,
        in_specs=[near] + [afar] * len(inputs),
        out_specs=[near] * len(shapes),
        scratch_shapes=scratch,
        compiler_params=pltpu.CompilerParams(vmem_limit_bytes=8 << 20),
        cost_estimate=COST,
        name="stage",
    )(ready, *inputs)
    keep(stages, arrays)
    stages = [("z", 1)] if last_piece > 0 else []
    which, inputs, shapes, scratch = staged_of(stages)
    left, b_turned, *arrays = pl.pallas_call(
        functools.partial(groups_kernel, groups, which),
        out_shape=[
            jax.ShapeDtypeStruct((groups, length, sub_width), BF16),
            jax.ShapeDtypeStruct((groups, STATE, length), BF16),
        ] + shapes,
        in_specs=[near] * 4 + [afar] * len(inputs),
        out_specs=[near] * (2 + len(shapes)),
        scratch_shapes=scratch or [pltpu.SemaphoreType.DMA((1,))],
        compiler_params=pltpu.CompilerParams(vmem_limit_bytes=12 << 20),
        cost_estimate=COST,
        name="groups",
    )(bc_flat, early, taps_bc, lines, *inputs)
    keep(stages, arrays)

    def local(chunk, gate, stages):
        group, piece = chunk // in_group, chunk * CHUNK // PIECE
        which, inputs, shapes, scratch = staged_of(stages)
        result = pl.pallas_call(
            functools.partial(local_kernel, group, chunk, which),
            in_specs=[near] * 10 + [afar] * len(inputs),
            out_specs=[near] * (4 + len(shapes)),
            out_shape=[
                jax.ShapeDtypeStruct((length, CHUNK), F32),
                jax.ShapeDtypeStruct((length, CHUNK), F32),
                jax.ShapeDtypeStruct((STATE, CHUNK), F32),
                jax.ShapeDtypeStruct((line_rows, CHUNK), F32),
            ] + shapes,
            scratch_shapes=scratch,
            compiler_params=pltpu.CompilerParams(vmem_limit_bytes=LOCAL_VMEM),
            cost_estimate=COST,
            name="local",
        )(
            pieces_x[piece], early, taps_x, pieces_z[piece], left, b_turned, grow, shrink, lines,
            gate, *inputs,
        )
        keep(stages, result[4:])
        return result[:4]

    def combine(owners, chunks, came, gate):
        lanes = [pieces[chunk][3] for chunk in chunks]
        states = [pieces[chunk][2] for chunk in chunks]
        return pl.pallas_call(
            functools.partial(combine_kernel, 2 * subs + 1, owners, len(came)),
            in_specs=[scalar] + [near] * (2 * len(owners) + len(came) + 1),
            out_specs=near,
            out_shape=hold,
            compiler_params=pltpu.CompilerParams(vmem_limit_bytes=8 << 20),
            cost_estimate=COST,
            name="combine",
        )(place, *lanes, *states, *came, gate)

    def absorb(chunk, owners, came, gate):
        part, reach = pieces[chunk][:2]
        return pl.pallas_call(
            functools.partial(absorb_kernel, chunk // in_group, chunk, owners),
            in_specs=[scalar] + [near] * (5 + len(came)),
            out_specs=(near, near),
            out_shape=(
                jax.ShapeDtypeStruct((length, CHUNK), F32),
                jax.ShapeDtypeStruct((length, 128), F32),
            ),
            compiler_params=pltpu.CompilerParams(vmem_limit_bytes=8 << 20),
            cost_estimate=COST,
            name="absorb",
        )(place, left, gain, part, reach, *came, gate)

    def finish(chunk, owners, came, done, out, gate):
        part, reach = pieces[chunk][:2]
        operands = [place, left, gain, part, reach, *came]
        operands += [pair[0] for pair in done] + [pair[1] for pair in done] + [gate]
        specs = [scalar] + [near] * (len(operands) - 1)
        aliases = {}
        if out is not None:
            aliases = {len(operands): 0}
            operands.append(far(out))
            specs.append(afar)
        return pl.pallas_call(
            functools.partial(finish_kernel, chunk // in_group, in_group, owners),
            in_specs=specs,
            out_specs=afar,
            out_shape=jax.ShapeDtypeStruct((length, channels), BF16),
            input_output_aliases=aliases,
            scratch_shapes=[
                pltpu.VMEM((length, per_group), BF16),
                pltpu.SemaphoreType.DMA((length // SUB * in_group,)),
            ],
            compiler_params=pltpu.CompilerParams(vmem_limit_bytes=12 << 20),
            cost_estimate=COST,
            name="finish",
        )(*operands)

    pieces, done = {}, []
    gate, out = b_turned, None

    def work(chunk):
        stages = []
        if len(pieces) < last_piece - 1:
            stages = [("x", len(pieces) + 2), ("z", len(pieces) + 2)]
        pieces[chunk] = local(chunk, gate, stages)
        return pieces[chunk][3]

    gate = first(1, gate, [])
    send(gate)
    gate = work(0)
    if count > 2:
        gate = first(2, gate, [])
        send(gate)
    last_step = count - 1 + 2 * max(hops - 2, 0)
    for step in range(last_step + 2):
        senders = [
            owner for owner in range(1, hops) if 0 <= step - 2 * (owner - 1) < count
        ]
        if senders:
            came = [from_first[step]] if step < count else []
            came += [from_later[step - 2]] if step >= 2 else []
            gate = combine(senders, [step - 2 * (owner - 1) for owner in senders], came, gate)
            from_later.append(
                lax.ppermute(gate, "ctx", [(owner, owner + 1) for owner in senders])
            )
        if step + 1 < count:
            gate = work(step + 1)
        if step + 3 < count:
            gate = first(step + 3, gate, [])
            send(gate)
        chunk = step - 1 - 2 * max(hops - 2, 0)
        if 0 <= chunk < count:
            owners = [0] + list(range(2, contexts))
            came = [from_first[chunk]] + [from_later[chunk + 2 * (i - 2)] for i in owners[1:]]
            if (chunk + 1) % in_group:
                done.append(absorb(chunk, owners, came, gate))
                gate = done[-1][1]
            else:
                out = finish(chunk, owners, came, done, out, gate)
                done = []
    return out


def solution(mesh):
    placed = (
        P(("groups", "ctx"), ("tp", "fsdp")),
        P(("groups", "ctx"), ("tp", "fsdp"), None),
        P(("groups", "ctx"), ("tp", "fsdp")),
        P(("groups", "ctx"), ("tp", "fsdp")),
        P(None, ("tp", "fsdp")),
        P(None, ("tp", "fsdp"), None),
        P(("tp", "fsdp")),
        P(("tp", "fsdp")),
        P(("tp", "fsdp")),
        P(("tp", "fsdp")),
    )
    return jax.shard_map(
        shards,
        mesh=mesh,
        in_specs=placed,
        out_specs=P(("groups", "ctx"), ("tp", "fsdp")),
        check_vma=False,
    )
```

```python
import functools

import jax
import jax.numpy as jnp
from jax import lax
from jax.experimental import pallas as pl
from jax.experimental.pallas import tpu as pltpu
from jax.sharding import PartitionSpec as P

HEAD_DIM = 64
STATE = 256
KERNEL = 4
SUB = 128
CHUNK = 512
PIECE = 2 * CHUNK
LOCAL_VMEM = 16 << 20
COST = pl.CostEstimate(flops=1 << 10, bytes_accessed=1 << 10, transcendentals=0)
F32 = jnp.float32
BF16 = jnp.bfloat16


def dot(left, right):
    return jnp.dot(left, right, preferred_element_type=F32)


def silu(value):
    half = 0.5 * value
    return half + half * jnp.tanh(half)


def two_terms(value):
    high = value.astype(BF16)
    low = (value - high.astype(F32)).astype(BF16)
    return high, low


def causal_conv(current, earlier, taps):
    length, width = current.shape
    wide = current.astype(F32)
    head = jnp.concatenate([jnp.zeros((8 - KERNEL + 1, width), F32), earlier.astype(F32)], axis=0)
    joined = jnp.concatenate([head, wide], axis=0)
    total = taps[KERNEL - 1 : KERNEL] * wide
    for back in range(1, KERNEL):
        row = KERNEL - 1 - back
        total = total + taps[row : row + 1] * joined[8 - back : 8 - back + length]
    return silu(total).astype(BF16)


def column_of(row):
    size = row.shape[1]
    at = lax.broadcasted_iota(jnp.int32, (size, size), 0)
    of = lax.broadcasted_iota(jnp.int32, (size, size), 1)
    return jnp.sum(jnp.where(at == of, row, 0.0), axis=1, keepdims=True)


def terms_by_row(value):
    high = value.astype(BF16).astype(F32)
    low = value - high
    return jnp.concatenate([high, low], axis=0).T.astype(BF16)


def started(pairs, sems):
    copies = [
        pltpu.make_async_copy(source, target, sems.at[index])
        for index, (source, target) in enumerate(pairs)
    ]
    for copy in copies:
        copy.start()
    return copies


def staging(stages, sources, targets, sems):
    return started(
        [
            (source.at[:, piece * PIECE : (piece + 1) * PIECE], target)
            for piece, source, target in zip(stages, sources, targets)
        ],
        sems,
    )


def steps_kernel(
    x_hbm, taps_x_hbm, taps_bc_hbm, bc_hbm, gain_hbm, dt_hbm, bias_hbm, rate_hbm, skip_hbm,
    x_ref, tail_ref, taps_x_ref, taps_bc_ref, bc_ref, gain_ref, u_ref, v_ref, rows_ref, *scratch
):
    small, (small_sems, whole_sems) = scratch[:4], scratch[4:]
    small_copies = started(zip((dt_hbm, bias_hbm, rate_hbm, skip_hbm), small), small_sems)
    tall, wide = x_ref.shape[0], x_ref.shape[1]
    whole_copies = started(
        (
            (x_hbm.at[tall - 8 : tall, :], tail_ref), (bc_hbm, bc_ref), (taps_bc_hbm, taps_bc_ref),
            (taps_x_hbm, taps_x_ref), (x_hbm.at[:, :wide], x_ref), (gain_hbm, gain_ref),
        ),
        whole_sems,
    )
    for copy in small_copies:
        copy.wait()
    dt_ref, bias_ref, rate_ref, skip_ref = small
    heads, length = dt_ref.shape
    shifted = dt_ref[...].astype(F32) + column_of(bias_ref[...])
    steps = jnp.maximum(shifted, 0.0) + jnp.log1p(jnp.exp(-jnp.abs(shifted)))
    log_decay = -jnp.exp(column_of(rate_ref[...])) * steps
    of = lax.broadcasted_iota(jnp.int32, (length, length), 0)
    at = lax.broadcasted_iota(jnp.int32, (length, length), 1)
    upper = jnp.where(at >= of, 1.0, 0.0).astype(BF16)
    first = log_decay.astype(BF16)
    rest = log_decay - first.astype(F32)
    second = rest.astype(BF16)
    third = (rest - second.astype(F32)).astype(BF16)
    cumulative = dot(first, upper) + dot(second, upper) + dot(third, upper)
    subs = length // SUB
    decays, scales = [], []
    start = jnp.zeros((heads, 1), F32)
    for sub in range(subs):
        rows = slice(sub * SUB, (sub + 1) * SUB)
        inside = cumulative[:, rows] - start
        u_ref[rows, :] = terms_by_row(jnp.exp(inside))
        v_ref[rows, :] = terms_by_row(jnp.exp(-inside) * steps[:, rows])
        end = cumulative[:, (sub + 1) * SUB - 1 : (sub + 1) * SUB]
        decays.append(jnp.exp(end - start))
        scales.append(jnp.exp(start))
        start = end
    lines = decays + scales + [column_of(skip_ref[...]), jnp.exp(start)]
    lane = lax.broadcasted_iota(jnp.int32, (heads, SUB), 1)
    table = jnp.zeros((heads, SUB), F32)
    for index, line in enumerate(lines):
        table = jnp.where(lane == index, line, table)
    rows_ref[...] = terms_by_row(table)[: rows_ref.shape[0]]
    for copy in whole_copies:
        copy.wait()


def stage_kernel(stages, gate_ref, *refs):
    for copy in staging(stages, refs[: len(stages)], refs[len(stages) : -1], refs[-1]):
        copy.wait()


def groups_kernel(groups, stages, bc_ref, early_ref, taps_ref, gate_ref, *refs):
    sources, (left_ref, bt_ref), targets = refs[: len(stages)], refs[len(stages) : len(stages) + 2], refs[len(stages) + 2 : -1]
    copies = staging(stages, sources, targets, refs[-1])
    length = bc_ref.shape[0]
    subs = length // SUB
    of = lax.broadcasted_iota(jnp.int32, (SUB, SUB), 1)
    at = lax.broadcasted_iota(jnp.int32, (SUB, SUB), 0)
    causal = at >= of
    for group in range(groups):
        lanes = slice(group * 2 * STATE, (group + 1) * 2 * STATE)
        base = early_ref.shape[1] - bc_ref.shape[1] + lanes.start
        earlier = early_ref[:, base : base + 2 * STATE]
        conv = causal_conv(bc_ref[:, lanes], earlier, taps_ref[:, group, :])
        b_turned = conv[:, :STATE].astype(F32).T.astype(BF16)
        c_rows = conv[:, STATE:]
        bt_ref[group] = b_turned
        for sub in range(subs):
            rows = slice(sub * SUB, (sub + 1) * SUB)
            scores = jnp.where(causal, dot(c_rows[rows], b_turned[:, rows]), 0.0)
            left_ref[group, rows, :SUB] = scores.astype(BF16)
            left_ref[group, rows, SUB:] = c_rows[rows]
    for copy in copies:
        copy.wait()


def spread_matrix(terms, width, first_head):
    row = lax.broadcasted_iota(jnp.int32, (terms, width), 0)
    lane = lax.broadcasted_iota(jnp.int32, (terms, width), 1)
    heads = terms // 2
    start = (jnp.where(row >= heads, row - heads, row) - first_head) * HEAD_DIM
    return jnp.where((lane >= start) & (lane < start + HEAD_DIM), 1.0, 0.0).astype(BF16)


def next_state(state, scaled, b_turned, decay):
    added = dot(b_turned, scaled)
    return decay * (added if state is None else state + added)


def first_kernel(
    group, chunk, stages, place_ref, x_ref, taps_ref, v_ref, rows_ref, bc_ref, bc_taps_ref, gate_ref, *refs
):
    send_ref = refs[len(stages)]
    copies = staging(stages, refs[: len(stages)], refs[len(stages) + 1 : -1], refs[-1]) if stages else []

    @pl.when(place_ref[0] == 0)
    def _():
        at = slice(chunk * CHUNK, (chunk + 1) * CHUNK)
        length, width = x_ref.shape[0], CHUNK
        spread = spread_matrix(v_ref.shape[1], width, chunk * (CHUNK // HEAD_DIM))
        lanes = dot(rows_ref[...], spread)
        start = group * 2 * STATE
        nothing = jnp.zeros((KERNEL - 1, STATE), BF16)
        b_rows = causal_conv(bc_ref[:, start : start + STATE], nothing, bc_taps_ref[:, group, :STATE])
        b_turned = b_rows.astype(F32).T.astype(BF16)
        nothing = jnp.zeros((KERNEL - 1, width), BF16)
        inner_at = slice(chunk * CHUNK % PIECE, chunk * CHUNK % PIECE + CHUNK)
        conv = causal_conv(x_ref[:, inner_at], nothing, taps_ref[:, at])
        state = None
        for sub in range(length // SUB):
            rows = slice(sub * SUB, (sub + 1) * SUB)
            scaled = (conv[rows].astype(F32) * dot(v_ref[rows], spread)).astype(BF16)
            state = next_state(state, scaled, b_turned[:, rows], lanes[sub : sub + 1])
        send_ref[...] = state.astype(send_ref.dtype)

    for copy in copies:
        copy.wait()


def local_kernel(
    group, chunk, stages, x_ref, early_ref, taps_ref, z_ref, left_ref, bt_ref, u_ref, v_ref, rows_ref,
    gate_ref, *refs
):
    outs = len(stages)
    part_ref, reach_ref, state_ref, lanes_ref = refs[outs : outs + 4]
    copies = staging(stages, refs[:outs], refs[outs + 4 : -1], refs[-1]) if stages else []
    lanes_at = slice(chunk * CHUNK, (chunk + 1) * CHUNK)
    inner_at = slice(chunk * CHUNK % PIECE, chunk * CHUNK % PIECE + CHUNK)
    length, width = x_ref.shape[0], CHUNK
    spread = spread_matrix(u_ref.shape[1], width, chunk * (CHUNK // HEAD_DIM))
    lanes = dot(rows_ref[...], spread)
    lanes_ref[...] = lanes
    conv = causal_conv(x_ref[:, inner_at], early_ref[:, lanes_at], taps_ref[:, lanes_at])
    subs = length // SUB
    skip = lanes[2 * subs : 2 * subs + 1]
    state = None
    for sub in range(subs):
        rows = slice(sub * SUB, (sub + 1) * SUB)
        inputs = conv[rows].astype(F32)
        scaled = (inputs * dot(v_ref[rows], spread)).astype(BF16)
        inner = dot(left_ref[group, rows, :SUB], scaled)
        if sub > 0:
            inner = inner + dot(left_ref[group, rows, SUB:], state.astype(BF16))
        state = next_state(state, scaled, bt_ref[group, :, rows], lanes[sub : sub + 1])
        grown = dot(u_ref[rows], spread)
        gate = silu(z_ref[rows, inner_at].astype(F32))
        part_ref[rows, :] = gate * (grown * inner + skip * inputs)
        reach_ref[rows, :] = gate * grown * lanes[subs + sub : subs + sub + 1]
    state_ref[...] = state
    for copy in copies:
        copy.wait()


def combine_kernel(line, owners, arrivals, place_ref, *refs):
    place = place_ref[0]
    lanes = refs[: len(owners)]
    states = refs[len(owners) : 2 * len(owners)]
    came = refs[2 * len(owners) : 2 * len(owners) + arrivals]
    sent_ref = refs[-1]
    total, state = lanes[0][line : line + 1], states[0][...]
    for owner, lane_ref, state_ref in zip(owners[1:], lanes[1:], states[1:]):
        total = jnp.where(place >= owner, lane_ref[line : line + 1], total)
        state = jnp.where(place >= owner, state_ref[...], state)
    value = came[0][...].astype(F32)
    for other in came[1:]:
        value = jnp.where(place >= 2, other[...].astype(F32), value)
    sent_ref[...] = (total * value + state).astype(sent_ref.dtype)


def arrived_state(place, owners, refs):
    incoming = refs[0][...].astype(F32)
    for owner, other in zip(owners[1:], refs[1:]):
        incoming = jnp.where(place >= owner, other[...].astype(F32), incoming)
    return incoming.astype(BF16)


def absorb_kernel(group, chunk, owners, place_ref, left_ref, gain_ref, part_ref, reach_ref, *refs):
    length, width = part_ref.shape
    gated_ref, square_ref = refs[-2:]
    incoming = arrived_state(place_ref[0], owners, refs[: len(owners)])
    gain = gain_ref[:, chunk * CHUNK : (chunk + 1) * CHUNK]
    for start in range(0, length, SUB):
        rows = slice(start, start + SUB)
        value = part_ref[rows] + reach_ref[rows] * dot(left_ref[group, rows, SUB:], incoming)
        gated_ref[rows, :] = value * gain
        power = value * value
        total = power[:, :128]
        for lane in range(128, width, 128):
            total = total + power[:, lane : lane + 128]
        square_ref[rows, :] = total


def finish_kernel(group, chunks, owners, place_ref, left_ref, gain_ref, part_ref, reach_ref, *refs):
    length, width = part_ref.shape
    came, refs = refs[: len(owners)], refs[len(owners) :]
    gated, squares = refs[: chunks - 1], refs[chunks - 1 : 2 * chunks - 2]
    out_hbm, out_ref, sems = refs[-3:]
    incoming = arrived_state(place_ref[0], owners, came)
    first_lane = group * chunks * width
    last = slice(first_lane + (chunks - 1) * width, first_lane + chunks * width)
    copies = []
    for start in range(0, length, SUB):
        rows = slice(start, start + SUB)
        value = part_ref[rows] + reach_ref[rows] * dot(left_ref[group, rows, SUB:], incoming)
        square = jnp.sum(value * value, axis=1, keepdims=True)
        if chunks > 1:
            total = squares[0][rows]
            for other in squares[1:]:
                total = total + other[rows]
            square = square + jnp.sum(total, axis=1, keepdims=True)
        scale = lax.rsqrt(square * (1.0 / (width * chunks)) + 1e-05)
        for index in range(chunks):
            scaled = value * gain_ref[:, last] if index == chunks - 1 else gated[index][rows]
            lanes = slice(index * width, (index + 1) * width)
            out_ref[rows, lanes] = (scaled * scale).astype(BF16)
            copies.append(
                pltpu.make_async_copy(
                    out_ref.at[rows, lanes],
                    out_hbm.at[rows, first_lane + index * width : first_lane + (index + 1) * width],
                    sems.at[len(copies)],
                )
            )
            copies[-1].start()
    for copy in copies:
        copy.wait()


def shards(x_in, bc_in, z_in, dt_in, conv_x, conv_bc, dt_bias, a_log, d_skip, norm_gain):
    length, channels = x_in.shape
    groups = bc_in.shape[1]
    heads = channels // HEAD_DIM
    contexts = lax.axis_size("ctx")
    wire = BF16 if contexts <= 8 else F32
    margin = KERNEL - 1
    subs = length // SUB
    ahead = [(i, i + 1) for i in range(contexts - 1)]
    bc_width = groups * 2 * STATE
    line_rows = -(-(2 * subs + 2) // 8) * 8
    sub_width = SUB + STATE
    place = lax.axis_index("ctx").astype(jnp.int32).reshape(1)
    small = (dt_in.T, dt_bias.reshape(1, heads), a_log.reshape(1, heads), d_skip.reshape(1, heads))
    far = lambda array: pltpu.with_memory_space_constraint(array, pltpu.HBM)
    large = tuple(far(array) for array in (x_in, conv_x, conv_bc, bc_in, norm_gain.reshape(1, channels)))
    begun = PIECE
    x_begun, tail, taps_x, taps_bc, bc_near, gain, grow, shrink, lines = pl.pallas_call(
        steps_kernel,
        in_specs=[pl.BlockSpec(memory_space=pltpu.HBM)] * (len(large) + len(small)),
        out_specs=[pl.BlockSpec(memory_space=pltpu.VMEM)] * 9,
        out_shape=(
            jax.ShapeDtypeStruct((length, begun), BF16),
            jax.ShapeDtypeStruct((8, channels), BF16),
            jax.ShapeDtypeStruct(conv_x.shape, F32),
            jax.ShapeDtypeStruct(conv_bc.shape, F32),
            jax.ShapeDtypeStruct(bc_in.shape, BF16),
            jax.ShapeDtypeStruct((1, channels), F32),
            jax.ShapeDtypeStruct((length, 2 * heads), BF16),
            jax.ShapeDtypeStruct((length, 2 * heads), BF16),
            jax.ShapeDtypeStruct((line_rows, 2 * heads), BF16),
        ),
        scratch_shapes=[pltpu.VMEM(array.shape, array.dtype) for array in small] + [
            pltpu.SemaphoreType.DMA((len(small),)), pltpu.SemaphoreType.DMA((6,)),
        ],
        compiler_params=pltpu.CompilerParams(vmem_limit_bytes=12 << 20),
        cost_estimate=COST,
        name="steps",
    )(*large, *[far(array) for array in small])
    bc_flat = bc_near.reshape(length, bc_width)
    per_group = channels // groups
    in_group = per_group // CHUNK
    count = channels // CHUNK
    hops = contexts - 1
    near = pl.BlockSpec(memory_space=pltpu.VMEM)
    scalar = pl.BlockSpec(memory_space=pltpu.SMEM)
    afar = pl.BlockSpec(memory_space=pltpu.HBM)
    last_piece = channels // PIECE - 1
    hold = jax.ShapeDtypeStruct((STATE, CHUNK), wire)
    from_first, from_later = [], []

    def send(value):
        from_first.append(lax.ppermute(value, "ctx", [(0, 1)]))

    pieces_x, pieces_z = {0: x_begun}, {}
    z_far = far(z_in)

    def staged_of(stages):
        inputs = [large[0] if name == "x" else z_far for name, _ in stages]
        shapes = [jax.ShapeDtypeStruct((length, PIECE), BF16) for _ in stages]
        scratch = [pltpu.SemaphoreType.DMA((len(stages),))] if stages else []
        return [piece for _, piece in stages], inputs, shapes, scratch

    def keep(stages, arrays):
        for (name, piece), array in zip(stages, arrays):
            (pieces_x if name == "x" else pieces_z)[piece] = array

    def first(chunk, gate, stages):
        which, inputs, shapes, scratch = staged_of(stages)
        result = pl.pallas_call(
            functools.partial(first_kernel, chunk // in_group, chunk, which),
            in_specs=[scalar] + [near] * 7 + [afar] * len(inputs),
            out_specs=[near] * (1 + len(shapes)),
            out_shape=[hold] + shapes,
            scratch_shapes=scratch,
            compiler_params=pltpu.CompilerParams(vmem_limit_bytes=12 << 20),
            cost_estimate=COST,
            name="first",
        )(place, pieces_x[chunk * CHUNK // PIECE], taps_x, shrink, lines, bc_flat, taps_bc, gate, *inputs)
        keep(stages, result[1:])
        return result[0]

    early = jnp.concatenate([tail[-margin:], bc_near[-margin:].reshape(margin, bc_width)], axis=1)
    ready = first(0, shrink, [])
    early, ready = lax.optimization_barrier((early, ready))
    early = lax.ppermute(early, "ctx", ahead)
    send(ready)
    stages = [("z", 0)]
    which, inputs, shapes, scratch = staged_of(stages)
    arrays = pl.pallas_call(
        functools.partial(stage_kernel, which),
        out_shape=shapes,
        in_specs=[near] + [afar] * len(inputs),
        out_specs=[near] * len(shapes),
        scratch_shapes=scratch,
        compiler_params=pltpu.CompilerParams(vmem_limit_bytes=8 << 20),
        cost_estimate=COST,
        name="stage",
    )(ready, *inputs)
    keep(stages, arrays)
    stages = [("x", 1)] if last_piece > 0 else []
    which, inputs, shapes, scratch = staged_of(stages)
    left, b_turned, *arrays = pl.pallas_call(
        functools.partial(groups_kernel, groups, which),
        out_shape=[
            jax.ShapeDtypeStruct((groups, length, sub_width), BF16),
            jax.ShapeDtypeStruct((groups, STATE, length), BF16),
        ] + shapes,
        in_specs=[near] * 4 + [afar] * len(inputs),
        out_specs=[near] * (2 + len(shapes)),
        scratch_shapes=scratch or [pltpu.SemaphoreType.DMA((1,))],
        compiler_params=pltpu.CompilerParams(vmem_limit_bytes=12 << 20),
        cost_estimate=COST,
        name="groups",
    )(bc_flat, early, taps_bc, lines, *inputs)
    keep(stages, arrays)

    def local(chunk, gate, stages):
        group, piece = chunk // in_group, chunk * CHUNK // PIECE
        which, inputs, shapes, scratch = staged_of(stages)
        result = pl.pallas_call(
            functools.partial(local_kernel, group, chunk, which),
            in_specs=[near] * 10 + [afar] * len(inputs),
            out_specs=[near] * (4 + len(shapes)),
            out_shape=[
                jax.ShapeDtypeStruct((length, CHUNK), F32),
                jax.ShapeDtypeStruct((length, CHUNK), F32),
                jax.ShapeDtypeStruct((STATE, CHUNK), F32),
                jax.ShapeDtypeStruct((line_rows, CHUNK), F32),
            ] + shapes,
            scratch_shapes=scratch,
            compiler_params=pltpu.CompilerParams(vmem_limit_bytes=LOCAL_VMEM),
            cost_estimate=COST,
            name="local",
        )(
            pieces_x[piece], early, taps_x, pieces_z[piece], left, b_turned, grow, shrink, lines,
            gate, *inputs,
        )
        keep(stages, result[4:])
        return result[:4]

    def combine(owners, chunks, came, gate):
        lanes = [pieces[chunk][3] for chunk in chunks]
        states = [pieces[chunk][2] for chunk in chunks]
        return pl.pallas_call(
            functools.partial(combine_kernel, 2 * subs + 1, owners, len(came)),
            in_specs=[scalar] + [near] * (2 * len(owners) + len(came) + 1),
            out_specs=near,
            out_shape=hold,
            compiler_params=pltpu.CompilerParams(vmem_limit_bytes=8 << 20),
            cost_estimate=COST,
            name="combine",
        )(place, *lanes, *states, *came, gate)

    def absorb(chunk, owners, came, gate):
        part, reach = pieces[chunk][:2]
        return pl.pallas_call(
            functools.partial(absorb_kernel, chunk // in_group, chunk, owners),
            in_specs=[scalar] + [near] * (5 + len(came)),
            out_specs=(near, near),
            out_shape=(
                jax.ShapeDtypeStruct((length, CHUNK), F32),
                jax.ShapeDtypeStruct((length, 128), F32),
            ),
            compiler_params=pltpu.CompilerParams(vmem_limit_bytes=8 << 20),
            cost_estimate=COST,
            name="absorb",
        )(place, left, gain, part, reach, *came, gate)

    def finish(chunk, owners, came, done, out, gate):
        part, reach = pieces[chunk][:2]
        operands = [place, left, gain, part, reach, *came]
        operands += [pair[0] for pair in done] + [pair[1] for pair in done] + [gate]
        specs = [scalar] + [near] * (len(operands) - 1)
        aliases = {}
        if out is not None:
            aliases = {len(operands): 0}
            operands.append(far(out))
            specs.append(afar)
        return pl.pallas_call(
            functools.partial(finish_kernel, chunk // in_group, in_group, owners),
            in_specs=specs,
            out_specs=afar,
            out_shape=jax.ShapeDtypeStruct((length, channels), BF16),
            input_output_aliases=aliases,
            scratch_shapes=[
                pltpu.VMEM((length, per_group), BF16),
                pltpu.SemaphoreType.DMA((length // SUB * in_group,)),
            ],
            compiler_params=pltpu.CompilerParams(vmem_limit_bytes=12 << 20),
            cost_estimate=COST,
            name="finish",
        )(*operands)

    pieces, done = {}, []
    gate, out = b_turned, None

    def work(chunk):
        stages = [("z", len(pieces) + 1), ("x", len(pieces) + 2)]
        stages = [(name, piece) for name, piece in stages if piece <= last_piece]
        pieces[chunk] = local(chunk, gate, stages)
        return pieces[chunk][3]

    gate = first(1, gate, [])
    send(gate)
    gate = work(0)
    if count > 2:
        gate = first(2, gate, [])
        send(gate)
    last_step = count - 1 + 2 * max(hops - 2, 0)
    for step in range(last_step + 2):
        senders = [
            owner for owner in range(1, hops) if 0 <= step - 2 * (owner - 1) < count
        ]
        if senders:
            came = [from_first[step]] if step < count else []
            came += [from_later[step - 2]] if step >= 2 else []
            gate = combine(senders, [step - 2 * (owner - 1) for owner in senders], came, gate)
            from_later.append(
                lax.ppermute(gate, "ctx", [(owner, owner + 1) for owner in senders])
            )
        if step + 1 < count:
            gate = work(step + 1)
        if step + 3 < count:
            gate = first(step + 3, gate, [])
            send(gate)
        chunk = step - 1 - 2 * max(hops - 2, 0)
        if 0 <= chunk < count:
            owners = [0] + list(range(2, contexts))
            came = [from_first[chunk]] + [from_later[chunk + 2 * (i - 2)] for i in owners[1:]]
            if (chunk + 1) % in_group:
                done.append(absorb(chunk, owners, came, gate))
                gate = done[-1][1]
            else:
                out = finish(chunk, owners, came, done, out, gate)
                done = []
    return out


def solution(mesh):
    placed = (
        P(("groups", "ctx"), ("tp", "fsdp")),
        P(("groups", "ctx"), ("tp", "fsdp"), None),
        P(("groups", "ctx"), ("tp", "fsdp")),
        P(("groups", "ctx"), ("tp", "fsdp")),
        P(None, ("tp", "fsdp")),
        P(None, ("tp", "fsdp"), None),
        P(("tp", "fsdp")),
        P(("tp", "fsdp")),
        P(("tp", "fsdp")),
        P(("tp", "fsdp")),
    )
    return jax.shard_map(
        shards,
        mesh=mesh,
        in_specs=placed,
        out_specs=P(("groups", "ctx"), ("tp", "fsdp")),
        check_vma=False,
    )
```
